128 devices in a mesh: segment: 4 (over y), lane: 32 (over x, z, core).
Axes of the slice: x: 4, y: 4, z: 4, core: 2. Of those that a mesh axis runs over, the one named last changes fastest.
Arguments:
- frames: bfloat16 [96, 197, 1024], P('lane'), may hold values from -6 to 6
- triple_weight: bfloat16 [4, 1024, 3072], P('segment'), as said below
- output_weight: bfloat16 [4, 1024, 1024], P('segment'), may hold values from -0.1875 to 0.1875
- expand_weight: bfloat16 [4, 1024, 4096], P('segment', None, 'lane'), may hold values from -0.1875 to 0.1875
- reduce_weight: bfloat16 [4, 4096, 1024], P('segment', 'lane'), may hold values from -0.09375 to 0.09375
- attend_gain: float32 [4, 1024], P('segment'), may hold values from 0.1 to 1.9
- dense_gain: float32 [4, 1024], P('segment'), may hold values from 0.1 to 1.9
- final_gain: float32 [1024], replicated, may hold values from 0.1 to 1.9
- shot_lengths: int32 [24], replicated, may hold values from 1 to 12, as said below
Outputs:
- shot_frames: float32 [96, 1024], P('lane', 'segment')
The draws below stay inside these ranges and needn't reach their ends.
Inputs may be any that keep to these rules, and one draw needn't show every extreme that they name: `shot_lengths`: each shot is a run of consecutive frames; the lengths sum to 96; the first shot has 2 frames and the second exactly 12. `triple_weight`: query and value columns are drawn like a weight with fan-in 1024; key columns may be up to 60 times that scale and correlated with the query columns.
All inputs are finite; a program needn't handle non-finite values.
Results may differ from the reference program's by a relative error of at most 0.023.
Values may be sent and summed in bfloat16 or wider, within the bound.
A program may use at most 128 MiB of HBM per device.

```python
import math
import jax
import jax.numpy as jnp
from jax import lax

D = 1024
HEADS = 16
FF = 4096
PATCH = 197
FR_DEV = 3
MOST = 12
LAYERS = 4
FRAMES = 96
SHOTS = 24


def draw_triple_weight(key, part):
    first_key = jax.random.fold_in(key, 11)
    drawn = jax.random.normal(first_key, (LAYERS, D, 3 * D), jnp.float32) * D ** (-0.5)
    return drawn.astype(jnp.bfloat16)


def draw_shot_lengths(key, part):
    base_key = jax.random.fold_in(key, 21)
    remaining = SHOTS - 2
    extra_frames = FRAMES - MOST - FR_DEV + 1 - remaining
    indices = jnp.arange(remaining, dtype=jnp.int32)

    def place(step, lengths):
        scores = jax.random.randint(jax.random.fold_in(base_key, step), (remaining,), 0, 65536, dtype=jnp.int32) * remaining + indices
        scores = jnp.where(lengths < MOST, scores, -1)
        chosen = jnp.argmax(scores).astype(jnp.int32)
        return lengths + (indices == chosen).astype(jnp.int32)
    lengths = lax.fori_loop(0, extra_frames, place, jnp.ones((remaining,), jnp.int32))
    leading = jnp.array([FR_DEV - 1, MOST], dtype=jnp.int32)
    return jnp.concatenate([leading, lengths], axis=0)


def block_levels(rng, shape, pieces, least, top_value):
    def one(dim, parts):
        heights = jax.random.uniform(jax.random.fold_in(jax.random.fold_in(rng, 6), dim), (parts,), jnp.float32, least / len(pieces), top_value / len(pieces))
        return jnp.repeat(jnp.exp(heights), shape[dim] // parts).reshape((-1,) + (1,) * (len(shape) - dim - 1))

    factor_of = one(*pieces[0])
    for cut in pieces[1:]:
        factor_of = factor_of * one(*cut)
    return factor_of


def normal_values(rng, dims, scale, limit, cuts=(), held_as=jnp.bfloat16):
    entries = scale * jax.random.normal(rng, dims, jnp.float32)
    if cuts:
        entries = entries * block_levels(rng, dims, cuts, -0.22, 0.18)
    return jnp.clip(entries, -limit, limit).astype(held_as)


def setup_inputs(seed: int = 0) -> dict:
    arg_keys = jax.random.split(jax.random.key(seed), 10)
    frames = normal_values(arg_keys[0], (FRAMES, PATCH, D), 1.0, 6.0, ((0, 32),))
    triple_weight = draw_triple_weight(jax.random.fold_in(arg_keys[9], 71), 0)
    output_weight = normal_values(arg_keys[2], (LAYERS, D, D), D ** -0.5, 0.1875, ((0, 4),))
    expand_weight = normal_values(arg_keys[3], (LAYERS, D, FF), D ** -0.5, 0.1875, ((0, 4), (2, 32)))
    reduce_weight = normal_values(arg_keys[4], (LAYERS, FF, D), FF ** -0.5, 0.09375, ((0, 4), (1, 32)))
    attend_gain = jnp.clip(1.0 + 0.18 * jax.random.normal(arg_keys[5], (LAYERS, D), jnp.float32), 0.1, 1.9)
    dense_gain = jnp.clip(1.0 + 0.18 * jax.random.normal(arg_keys[6], (LAYERS, D), jnp.float32), 0.1, 1.9)
    final_gain = jnp.clip(1.0 + 0.18 * jax.random.normal(arg_keys[7], (D,), jnp.float32), 0.1, 1.9)
    shot_lengths = draw_shot_lengths(jax.random.fold_in(arg_keys[9], 71), 0)
    return dict(frames=frames, triple_weight=triple_weight, output_weight=output_weight, expand_weight=expand_weight, reduce_weight=reduce_weight, attend_gain=attend_gain, dense_gain=dense_gain, final_gain=final_gain, shot_lengths=shot_lengths)


def rounded(values):
    return lax.optimization_barrier(values.astype(jnp.bfloat16)).astype(jnp.float32)

def product(left_side, right_side):
    return jnp.dot(left_side.astype(jnp.float32), right_side.astype(jnp.float32), precision=lax.Precision.HIGHEST)

def normalize(states, gain_row):
    average = lax.optimization_barrier(jnp.mean(states, axis=-1, keepdims=True))
    centred = states - average
    spread = lax.optimization_barrier(jnp.mean(centred * centred, axis=-1, keepdims=True))
    return centred * lax.rsqrt(spread + 1e-06) * gain_row

def spatial_layer(states, triple_weight, output_weight, expand_weight, reduce_weight, attend_gain, dense_gain):
    row_count, model_width = states.shape
    head_size = model_width // HEADS
    normed = rounded(normalize(states, attend_gain))
    packed = rounded(product(normed, triple_weight)).reshape(row_count, 3, HEADS, head_size)
    scores = jnp.einsum('qhe,khe->hqk', packed[:, 0], packed[:, 1], precision=lax.Precision.HIGHEST) / math.sqrt(head_size)
    weights = rounded(jax.nn.softmax(scores, axis=-1))
    context = jnp.einsum('hqk,khe->qhe', weights, packed[:, 2], precision=lax.Precision.HIGHEST)
    context = rounded(context.reshape(row_count, model_width))
    states = states + product(context, output_weight)
    normed = rounded(normalize(states, dense_gain))
    hidden = rounded(jax.nn.gelu(product(normed, expand_weight), approximate=False))
    return states + product(hidden, reduce_weight)

def reference(frames, triple_weight, output_weight, expand_weight, reduce_weight, attend_gain, dense_gain, final_gain, shot_lengths):

    def encode(frame_rows):
        states = frame_rows.astype(jnp.float32)
        for layer in range(LAYERS - 1):
            states = spatial_layer(states, triple_weight[layer], output_weight[layer], expand_weight[layer], reduce_weight[layer], attend_gain[layer], dense_gain[layer])
        return lax.optimization_barrier(jnp.mean(normalize(states, final_gain), axis=0))
    pooled = lax.map(encode, frames)
    shot_ends = jnp.cumsum(shot_lengths).astype(jnp.int32)
    positions = jnp.arange(FRAMES, dtype=jnp.int32)
    shot_of = lax.optimization_barrier(jnp.sum((shot_ends[None, :] <= positions[:, None]).astype(jnp.int32), axis=1))
    same_shot = shot_of[:, None] == shot_of[None, :]
    last_layer = LAYERS - 1
    model_width = pooled.shape[1]
    head_size = model_width // HEADS
    normed = rounded(normalize(pooled, attend_gain[last_layer]))
    packed = rounded(product(normed, triple_weight[last_layer])).reshape(FRAMES, 3, HEADS, head_size)
    scores = jnp.einsum('qhe,khe->hqk', packed[:, 0], packed[:, 1], precision=lax.Precision.HIGHEST) / math.sqrt(head_size)
    scores = jnp.where(same_shot[None], scores, -jnp.inf)
    weights = jax.nn.softmax(scores, axis=-1)
    context = jnp.einsum('hqk,khe->qhe', weights, packed[:, 2], precision=lax.Precision.HIGHEST)
    context = rounded(context.reshape(FRAMES, model_width))
    temporal = pooled + product(context, output_weight[last_layer])
    normed = rounded(normalize(temporal, dense_gain[last_layer]))
    hidden = rounded(jax.nn.gelu(product(normed, expand_weight[last_layer]), approximate=False))
    return temporal + product(hidden, reduce_weight[last_layer])
```

```python
import functools
import math

import jax
import jax.numpy as jnp
from jax import lax
from jax.experimental import pallas as pl
from jax.experimental.pallas import tpu as pltpu
from jax.sharding import PartitionSpec as P

HEADS = 16
ROWS = 197
PAD = 208
D = 1024
FF = 4096
NF = 3
REACH = 4
SLOTS = 2 * REACH + 1
KEYS = 80
MESH = pl.DeviceIdType.MESH
F32 = jnp.float32
BF = jnp.bfloat16


def dot(a, b):
    return lax.dot_general(a, b, (((1,), (0,)), ((), ())), preferred_element_type=F32)


def dot_t(a, b):
    return lax.dot_general(a, b, (((1,), (1,)), ((), ())), preferred_element_type=F32)


def gelu(x):
    return 0.5 * x * (1.0 + lax.erf(x * (1.0 / math.sqrt(2.0))))


def norm_rows(x, gain):
    average = jnp.mean(x, axis=-1, keepdims=True)
    centred = x - average
    spread = jnp.mean(centred * centred, axis=-1, keepdims=True)
    return centred * lax.rsqrt(spread + 1e-06) * gain


def kernel(
    frames_ref, triple_hbm, output_hbm, expand_hbm, reduce_hbm, again_ref, dgain_ref, fgain_ref, shot_ref,
    out_ref,
    exp_v, red_v, trip_v, outw_v, state, inb, outb, packed, act, ctx, pooled, pin, obuf, rbuf,
    local_sem, send_sem, recv_sem, sib_send, sib_recv, rel_send, rel_recv, pool_send, pool_recv, fin_send, fin_recv,
):
    seg = lax.axis_index("segment")
    lane = lax.axis_index("lane")
    cx = lane // 8
    cz = (lane // 2) % 4
    core = lane % 2

    def lane_at(x, z, c):
        return ((x % 4) * 4 + (z % 4)) * 2 + c

    loads = [
        pltpu.make_async_copy(triple_hbm.at[0], trip_v, local_sem.at[0]),
        pltpu.make_async_copy(output_hbm.at[0], outw_v, local_sem.at[1]),
    ]
    for copy in loads:
        copy.start()

    peers = [
        (seg, lane_at(cx + 1, cz, core)), (seg, lane_at(cx + 3, cz, core)),
        (seg, lane_at(cx, cz + 1, core)), (seg, lane_at(cx, cz + 3, core)),
        (seg, lane_at(cx, cz, 1 - core)), ((seg + 2) % 4, lane),
    ]
    for d in range(-REACH, REACH + 1):
        peers.append(((seg + 1) % 4, (lane + d + 32) % 32))
        peers.append(((seg + 3) % 4, (lane - d + 32) % 32))
    barrier = pltpu.get_barrier_semaphore()
    for peer in peers:
        pl.semaphore_signal(barrier, inc=1, device_id=peer, device_id_type=MESH)
    pl.semaphore_wait(barrier, len(peers))

    def shard_lane(kind, dp, dq, c):
        if kind == 0:
            return lane_at(cx + dp + 4, cz + dq + 4, c)
        return lane_at(cx + dq + 4, cz + dp + 4, c)

    def region(kind, owner, half):
        if kind == 0:
            cols = pl.ds(pl.multiple_of(owner * 128, 128), 128)
            rows = pl.ds(0, D) if half is None else pl.ds(half * (D // 2), D // 2)
            return exp_v.at[rows, cols]
        if half is None:
            return red_v.at[pl.ds(pl.multiple_of(owner * 128, 128), 128), :]
        return red_v.at[pl.ds(pl.multiple_of(owner * 128 + half * 64, 64), 64), :]

    own_src = (expand_hbm.at[0], reduce_hbm.at[0])

    def neighbour(kind, along_p, sign):
        s = sign + 4
        if (kind == 0) == along_p:
            return (seg, lane_at(cx + s, cz, core))
        return (seg, lane_at(cx, cz + s, core))

    def hop(kind, dp, dq, half, along_p, sign):
        rp, rq = (dp - sign, dq) if along_p else (dp, dq - sign)
        h = half or 0
        dst = region(kind, shard_lane(kind, dp, dq, core), half)
        own = dp == 0 and dq == 0
        return pltpu.make_async_remote_copy(
            src_ref=own_src[kind] if own else dst, dst_ref=dst,
            send_sem=send_sem.at[kind, rp % 4, rq % 4, h], recv_sem=recv_sem.at[kind, rp % 4, rq % 4, h],
            device_id=neighbour(kind, along_p, sign), device_id_type=MESH)

    def arrival(kind, rp, rq, half):
        h = half or 0
        dst = region(kind, shard_lane(kind, rp, rq, core), half)
        return pltpu.make_async_remote_copy(
            src_ref=dst, dst_ref=dst,
            send_sem=send_sem.at[kind, rp % 4, rq % 4, h], recv_sem=recv_sem.at[kind, rp % 4, rq % 4, h],
            device_id=neighbour(kind, True, 1), device_id_type=MESH)

    def sibling(kind, dp, dq, receive=False):
        c = 1 - core if receive else core
        dst = region(kind, shard_lane(kind, dp, dq, c), None)
        own = dp == 0 and dq == 0 and not receive
        return pltpu.make_async_remote_copy(
            src_ref=own_src[kind] if own else dst, dst_ref=dst,
            send_sem=sib_send.at[kind, dp % 4, dq % 4], recv_sem=sib_recv.at[kind, dp % 4, dq % 4],
            device_id=(seg, lane_at(cx, cz, 1 - core)), device_id_type=MESH)

    sent = []

    def go(copy):
        copy.start()
        sent.append(copy)

    for kind in range(2):
        for sign in (1, -1):
            go(hop(kind, 0, 0, None, True, sign))
    for kind in range(2):
        for sign in (1, -1):
            go(hop(kind, 0, 0, None, False, sign))
        go(sibling(kind, 0, 0))
        mine = pltpu.make_async_copy(own_src[kind], region(kind, lane, None), local_sem.at[2 + kind])
        mine.start()
        loads.append(mine)

    def spread(kind, dp):
        for sign in (1, -1):
            go(hop(kind, dp, 0, None, False, sign))
        go(sibling(kind, dp, 0))

    def ev_p(kind, rp):
        arrival(kind, rp, 0, None).wait_recv()
        go(hop(kind, rp, 0, 0 if rp < 0 else 1, True, -rp))
        spread(kind, rp)

    def ev_p2(kind):
        arrival(kind, 2, 0, 0).wait_recv()
        arrival(kind, 2, 0, 1).wait_recv()
        spread(kind, 2)

    def ev_q(kind, rp, rq):
        arrival(kind, rp, rq, None).wait_recv()
        go(hop(kind, rp, rq, 0 if rq < 0 else 1, False, -rq))
        go(sibling(kind, rp, rq))

    def ev_q2(kind, rp):
        arrival(kind, rp, 2, 0).wait_recv()
        arrival(kind, rp, 2, 1).wait_recv()
        go(sibling(kind, rp, 2))

    events = []

    def both(fn, *args):
        for kind in range(2):
            events.append(functools.partial(fn, kind, *args))

    both(ev_p, -1)
    both(ev_p, 1)
    both(ev_q, 0, -1)
    both(ev_q, 0, 1)
    both(ev_p2)
    both(ev_q, -1, -1)
    both(ev_q, -1, 1)
    both(ev_q, 1, -1)
    both(ev_q, 1, 1)
    both(ev_q2, 0)
    both(ev_q, 2, -1)
    both(ev_q, 2, 1)
    both(ev_q2, -1)
    both(ev_q2, 1)
    both(ev_q2, 2)

    def norm_into(f, gain_ref):
        gain = gain_ref[...]
        for i in range(PAD // 16):
            rows = pl.ds(16 * i, 16)
            act[rows, :] = norm_rows(state[f, rows, :], gain).astype(BF)

    def project(f):
        norm_into(f, again_ref)

        def chunk(n, carry):
            cols = pl.ds(pl.multiple_of(n * 512, 512), 512)
            packed[:, cols] = dot(act[...], trip_v[:, cols]).astype(BF)
            return carry

        lax.fori_loop(0, 6, chunk, 0)

    def attend():
        low = lax.broadcasted_iota(jnp.int32, (PAD, 128), 1) < 64
        bias = jnp.where(lax.broadcasted_iota(jnp.int32, (1, PAD), 1) < ROWS, 0.0, -1e30).astype(F32)

        def pair(j, carry):
            at = pl.multiple_of(j * 128, 128)
            q = packed[:, pl.ds(at, 128)]
            k = packed[:, pl.ds(pl.multiple_of(at + D, 128), 128)]
            v = packed[:, pl.ds(pl.multiple_of(at + 2 * D, 128), 128)]
            parts = []
            for keep in (low, ~low):
                scores = dot_t(jnp.where(keep, q * 0.125, 0.0).astype(BF), k) + bias
                shares = jnp.exp(scores - jnp.max(scores, axis=-1, keepdims=True))
                total = jnp.sum(shares, axis=-1, keepdims=True)
                parts.append(dot(shares.astype(BF), v) / total)
            ctx[:, pl.ds(at, 128)] = jnp.where(low, parts[0], parts[1]).astype(BF)
            return carry

        lax.fori_loop(0, 8, pair, 0)

    def join(f):
        def chunk(n, carry):
            cols = pl.ds(pl.multiple_of(n * 512, 512), 512)
            state[f, :, cols] += dot(ctx[...], outw_v[:, cols])
            return carry

        lax.fori_loop(0, 2, chunk, 0)

    def feed(f):
        norm_into(f, dgain_ref)

        def chunk(n, carry):
            part = pl.ds(pl.multiple_of(n * 512, 512), 512)
            hidden = gelu(dot(act[...], exp_v[:, part])).astype(BF)
            state[f] += dot(hidden, red_v[part, :])
            return carry

        lax.fori_loop(0, 8, chunk, 0)

    for copy in loads[:2]:
        copy.wait()

    todo = list(events)

    def pump(count):
        for _ in range(min(count, len(todo))):
            todo.pop(0)()

    for f in range(NF):
        @pl.when(seg == 0)
        def _():
            state[f, 192:PAD, :] = jnp.zeros((PAD - 192, D), F32)
            state[f, 0:ROWS, :] = frames_ref[f].astype(F32)
            project(f)

        pump(4)

        @pl.when(seg == 0)
        def _():
            attend()

        pump(3)

        @pl.when(seg == 0)
        def _():
            join(f)

        pump(2)
    pump(len(todo))
    for kind in range(2):
        for dp in range(4):
            for dq in range(4):
                sibling(kind, dp, dq, receive=True).wait_recv()
    for copy in loads[2:]:
        copy.wait()

    def relay(f):
        return pltpu.make_async_remote_copy(
            src_ref=outb.at[f], dst_ref=inb.at[f], send_sem=rel_send.at[f], recv_sem=rel_recv.at[f],
            device_id=((seg + 1) % 4, lane), device_id_type=MESH)

    @pl.when(seg == 2)
    def _():
        pooled[...] = jnp.zeros_like(pooled)

    @pl.when(seg < 3)
    def _():
        def step(f, carry):
            @pl.when(seg > 0)
            def _():
                relay(f).wait_recv()
                state[f] = inb[f].astype(F32)
                project(f)
                attend()
                join(f)

            feed(f)

            @pl.when(seg < 2)
            def _():
                outb[f] = state[f].astype(BF)
                relay(f).start()

            @pl.when(seg == 2)
            def _():
                gain = fgain_ref[...]
                total = jnp.zeros((16, D), F32)
                for i in range(PAD // 16):
                    rows = norm_rows(state[f, pl.ds(16 * i, 16), :], gain)
                    if 16 * i + 16 > ROWS:
                        keep = lax.broadcasted_iota(jnp.int32, (16, D), 0) < ROWS - 16 * i
                        rows = jnp.where(keep, rows, 0.0)
                    total = total + rows
                pooled[pl.ds(f, 1), :] = jnp.sum(total, axis=0, keepdims=True) * (1.0 / ROWS)

            return carry

        lax.fori_loop(0, NF, step, 0)

    def pool_copy(d):
        return pltpu.make_async_remote_copy(
            src_ref=pooled, dst_ref=pin.at[pl.ds(8 * (d + REACH), 8), :],
            send_sem=pool_send.at[d + REACH], recv_sem=pool_recv.at[d + REACH],
            device_id=((seg + 1) % 4, (lane - d + 32) % 32), device_id_type=MESH)

    def result_copy(section):
        return pltpu.make_async_remote_copy(
            src_ref=obuf.at[section], dst_ref=rbuf, send_sem=fin_send.at[section], recv_sem=fin_recv,
            device_id=(section, lane), device_id_type=MESH)

    @pl.when(seg == 2)
    def _():
        for d in range(-REACH, REACH + 1):
            pool_copy(d).start()

    @pl.when(seg == 3)
    def _():
        pin[8 * SLOTS:KEYS, :] = jnp.zeros((KEYS - 8 * SLOTS, D), F32)
        for d in range(-REACH, REACH + 1):
            pool_copy(d).wait_recv()
        again = again_ref[...]
        for i in range(KEYS // 16):
            rows = pl.ds(16 * i, 16)
            act[rows, :] = norm_rows(pin[rows, :], again).astype(BF)

        def chunk(n, carry):
            cols = pl.ds(pl.multiple_of(n * 512, 512), 512)
            packed[0:KEYS, cols] = dot(act[0:KEYS, :], trip_v[:, cols]).astype(BF)
            return carry

        lax.fori_loop(0, 6, chunk, 0)

        col = lax.broadcasted_iota(jnp.int32, (16, KEYS), 1)
        row = lax.broadcasted_iota(jnp.int32, (16, KEYS), 0)
        key_lane = (lane + (col >> 3) - REACH + 32) & 31
        key_at = key_lane * NF + (col & 7)
        own_at = lane * NF + jnp.minimum(row, NF - 1)
        key_shot = jnp.zeros((16, KEYS), jnp.int32)
        own_shot = jnp.zeros((16, KEYS), jnp.int32)
        end = 0
        for s in range(24):
            end = end + shot_ref[s]
            key_shot += (key_at >= end).astype(jnp.int32)
            own_shot += (own_at >= end).astype(jnp.int32)
        allowed = (key_shot == own_shot) & ((col & 7) < NF) & (col < 8 * SLOTS)
        low = lax.broadcasted_iota(jnp.int32, (16, 128), 1) < 64
        mine = 8 * REACH

        def pair(j, carry):
            at = pl.multiple_of(j * 128, 128)
            q = packed[mine:mine + 16, pl.ds(at, 128)]
            k = packed[0:KEYS, pl.ds(pl.multiple_of(at + D, 128), 128)]
            v = packed[0:KEYS, pl.ds(pl.multiple_of(at + 2 * D, 128), 128)]
            parts = []
            for keep in (low, ~low):
                scores = dot_t(jnp.where(keep, q * 0.125, 0.0).astype(BF), k)
                scores = jnp.where(allowed, scores, -1e30)
                shares = jnp.exp(scores - jnp.max(scores, axis=-1, keepdims=True))
                total = jnp.sum(shares, axis=-1, keepdims=True)
                high = shares.astype(BF)
                rest = (shares - high.astype(F32)).astype(BF)
                parts.append((dot(high, v) + dot(rest, v)) / total)
            ctx[0:16, pl.ds(at, 128)] = jnp.where(low, parts[0], parts[1]).astype(BF)
            return carry

        lax.fori_loop(0, 8, pair, 0)
        temporal = pin[mine:mine + 16, :] + dot(ctx[0:16, :], outw_v[...])
        state[0, 0:16, :] = temporal
        act[0:16, :] = norm_rows(temporal, dgain_ref[...]).astype(BF)

        def ff_chunk(n, carry):
            part = pl.ds(pl.multiple_of(n * 512, 512), 512)
            hidden = gelu(dot(act[0:16, :], exp_v[:, part])).astype(BF)
            state[0, 0:16, :] += dot(hidden, red_v[part, :])
            return carry

        lax.fori_loop(0, 8, ff_chunk, 0)
        for section in range(4):
            obuf[section] = state[0, 0:8, 256 * section:256 * section + 256]
        for section in range(3):
            result_copy(section).start()
        out_ref[...] = obuf[3, 0:NF, :]
        for section in range(3):
            result_copy(section).wait_send()

    @pl.when(seg == 2)
    def _():
        for d in range(-REACH, REACH + 1):
            pool_copy(d).wait_send()

    @pl.when(seg < 2)
    def _():
        for f in range(NF):
            relay(f).wait_send()

    for copy in sent:
        copy.wait_send()

    @pl.when(seg < 3)
    def _():
        result_copy(0).wait_recv()
        out_ref[...] = rbuf[0:NF, :]


def body(frames, triple_weight, output_weight, expand_weight, reduce_weight, attend_gain, dense_gain, final_gain, shot_lengths):
    vmem = pl.BlockSpec(memory_space=pltpu.VMEM)
    anywhere = pl.BlockSpec(memory_space=pl.ANY)
    dma = pltpu.SemaphoreType.DMA
    return pl.pallas_call(
        kernel,
        out_shape=jax.ShapeDtypeStruct((NF, 256), F32),
        in_specs=[vmem, anywhere, anywhere, anywhere, anywhere, vmem, vmem, vmem,
                  pl.BlockSpec(memory_space=pltpu.SMEM)],
        out_specs=vmem,
        scratch_shapes=[
            pltpu.VMEM((D, FF), BF), pltpu.VMEM((FF, D), BF), pltpu.VMEM((D, 3 * D), BF), pltpu.VMEM((D, D), BF),
            pltpu.VMEM((NF, PAD, D), F32), pltpu.VMEM((NF, PAD, D), BF), pltpu.VMEM((NF, PAD, D), BF),
            pltpu.VMEM((PAD, 3 * D), BF), pltpu.VMEM((PAD, D), BF), pltpu.VMEM((PAD, D), BF),
            pltpu.VMEM((8, D), F32), pltpu.VMEM((KEYS, D), F32), pltpu.VMEM((4, 8, 256), F32), pltpu.VMEM((8, 256), F32),
            dma((4,)), dma((2, 4, 4, 2)), dma((2, 4, 4, 2)), dma((2, 4, 4)), dma((2, 4, 4)),
            dma((NF,)), dma((NF,)), dma((SLOTS,)), dma((SLOTS,)), dma((3,)), dma(()),
        ],
        compiler_params=pltpu.CompilerParams(
            collective_id=0, has_side_effects=True, vmem_limit_bytes=60 * 1024 * 1024),
    )(frames, triple_weight, output_weight, expand_weight, reduce_weight, attend_gain, dense_gain,
      final_gain.reshape(1, D), shot_lengths)


def solution(mesh):
    return jax.shard_map(
        body,
        mesh=mesh,
        in_specs=(
            P("lane", None, None),
            P("segment", None, None),
            P("segment", None, None),
            P("segment", None, "lane"),
            P("segment", "lane", None),
            P("segment", None),
            P("segment", None),
            P(),
            P(),
        ),
        out_specs=P("lane", "segment"),
        check_vma=False,
    )
```

```python
import functools
import math

import jax
import jax.numpy as jnp
from jax import lax
from jax.experimental import pallas as pl
from jax.experimental.pallas import tpu as pltpu
from jax.sharding import PartitionSpec as P

HEADS = 16
ROWS = 197
PAD = 208
D = 1024
FF = 4096
NF = 3
REACH = 4
SLOTS = 2 * REACH + 1
KEYS = 80
MESH = pl.DeviceIdType.MESH
F32 = jnp.float32
BF = jnp.bfloat16


def dot(a, b):
    return lax.dot_general(a, b, (((1,), (0,)), ((), ())), preferred_element_type=F32)


def dot_t(a, b):
    return lax.dot_general(a, b, (((1,), (1,)), ((), ())), preferred_element_type=F32)


def gelu(x):
    return 0.5 * x * (1.0 + lax.erf(x * (1.0 / math.sqrt(2.0))))


def norm_rows(x, gain):
    average = jnp.mean(x, axis=-1, keepdims=True)
    centred = x - average
    spread = jnp.mean(centred * centred, axis=-1, keepdims=True)
    return centred * lax.rsqrt(spread + 1e-06) * gain


def kernel(
    frames_ref, triple_hbm, output_hbm, expand_hbm, reduce_hbm, again_ref, dgain_ref, fgain_ref, shot_ref,
    out_ref,
    exp_v, red_v, trip_v, outw_v, state, inb, outb, packed, act, ctx, pooled, pin, obuf, rbuf,
    local_sem, send_sem, recv_sem, sib_send, sib_recv, rel_send, rel_recv, pool_send, pool_recv, fin_send, fin_recv,
):
    seg = lax.axis_index("segment")
    lane = lax.axis_index("lane")
    cx = lane // 8
    cz = (lane // 2) % 4
    core = lane % 2

    def lane_at(x, z, c):
        return ((x % 4) * 4 + (z % 4)) * 2 + c

    loads = [
        pltpu.make_async_copy(triple_hbm.at[0], trip_v, local_sem.at[0]),
        pltpu.make_async_copy(output_hbm.at[0], outw_v, local_sem.at[1]),
    ]
    for copy in loads:
        copy.start()

    peers = [
        (seg, lane_at(cx + 1, cz, core)), (seg, lane_at(cx + 3, cz, core)),
        (seg, lane_at(cx, cz + 1, core)), (seg, lane_at(cx, cz + 3, core)),
        (seg, lane_at(cx, cz, 1 - core)), ((seg + 2) % 4, lane),
    ]
    for d in range(-REACH, REACH + 1):
        peers.append(((seg + 1) % 4, (lane + d + 32) % 32))
        peers.append(((seg + 3) % 4, (lane - d + 32) % 32))
    barrier = pltpu.get_barrier_semaphore()
    for peer in peers:
        pl.semaphore_signal(barrier, inc=1, device_id=peer, device_id_type=MESH)
    pl.semaphore_wait(barrier, len(peers))

    def shard_lane(kind, dp, dq, c):
        if kind == 0:
            return lane_at(cx + dp + 4, cz + dq + 4, c)
        return lane_at(cx + dq + 4, cz + dp + 4, c)

    def region(kind, owner, half):
        if kind == 0:
            cols = pl.ds(pl.multiple_of(owner * 128, 128), 128)
            rows = pl.ds(0, D) if half is None else pl.ds(half * (D // 2), D // 2)
            return exp_v.at[rows, cols]
        if half is None:
            return red_v.at[pl.ds(pl.multiple_of(owner * 128, 128), 128), :]
        return red_v.at[pl.ds(pl.multiple_of(owner * 128 + half * 64, 64), 64), :]

    own_src = (expand_hbm.at[0], reduce_hbm.at[0])

    def neighbour(kind, along_p, sign):
        s = sign + 4
        if (kind == 0) == along_p:
            return (seg, lane_at(cx + s, cz, core))
        return (seg, lane_at(cx, cz + s, core))

    def hop(kind, dp, dq, half, along_p, sign):
        rp, rq = (dp - sign, dq) if along_p else (dp, dq - sign)
        h = half or 0
        dst = region(kind, shard_lane(kind, dp, dq, core), half)
        own = dp == 0 and dq == 0
        return pltpu.make_async_remote_copy(
            src_ref=own_src[kind] if own else dst, dst_ref=dst,
            send_sem=send_sem.at[kind, rp % 4, rq % 4, h], recv_sem=recv_sem.at[kind, rp % 4, rq % 4, h],
            device_id=neighbour(kind, along_p, sign), device_id_type=MESH)

    def arrival(kind, rp, rq, half):
        h = half or 0
        dst = region(kind, shard_lane(kind, rp, rq, core), half)
        return pltpu.make_async_remote_copy(
            src_ref=dst, dst_ref=dst,
            send_sem=send_sem.at[kind, rp % 4, rq % 4, h], recv_sem=recv_sem.at[kind, rp % 4, rq % 4, h],
            device_id=neighbour(kind, True, 1), device_id_type=MESH)

    def sibling(kind, dp, dq, receive=False):
        c = 1 - core if receive else core
        dst = region(kind, shard_lane(kind, dp, dq, c), None)
        own = dp == 0 and dq == 0 and not receive
        return pltpu.make_async_remote_copy(
            src_ref=own_src[kind] if own else dst, dst_ref=dst,
            send_sem=sib_send.at[kind, dp % 4, dq % 4], recv_sem=sib_recv.at[kind, dp % 4, dq % 4],
            device_id=(seg, lane_at(cx, cz, 1 - core)), device_id_type=MESH)

    sent = []

    def go(copy):
        copy.start()
        sent.append(copy)

    for kind in range(2):
        for sign in (1, -1):
            go(hop(kind, 0, 0, None, True, sign))
    for kind in range(2):
        for sign in (1, -1):
            go(hop(kind, 0, 0, None, False, sign))
        go(sibling(kind, 0, 0))
        mine = pltpu.make_async_copy(own_src[kind], region(kind, lane, None), local_sem.at[2 + kind])
        mine.start()
        loads.append(mine)

    def spread(kind, dp):
        for sign in (1, -1):
            go(hop(kind, dp, 0, None, False, sign))
        go(sibling(kind, dp, 0))

    def ev_p(kind, rp):
        arrival(kind, rp, 0, None).wait_recv()
        go(hop(kind, rp, 0, 0 if rp < 0 else 1, True, -rp))
        spread(kind, rp)

    def ev_p2(kind):
        arrival(kind, 2, 0, 0).wait_recv()
        arrival(kind, 2, 0, 1).wait_recv()
        spread(kind, 2)

    def ev_q(kind, rp, rq):
        arrival(kind, rp, rq, None).wait_recv()
        go(hop(kind, rp, rq, 0 if rq < 0 else 1, False, -rq))
        go(sibling(kind, rp, rq))

    def ev_q2(kind, rp):
        arrival(kind, rp, 2, 0).wait_recv()
        arrival(kind, rp, 2, 1).wait_recv()
        go(sibling(kind, rp, 2))

    events = []

    def both(fn, *args):
        for kind in range(2):
            events.append(functools.partial(fn, kind, *args))

    both(ev_p, -1)
    both(ev_p, 1)
    both(ev_q, 0, -1)
    both(ev_q, 0, 1)
    both(ev_p2)
    both(ev_q, -1, -1)
    both(ev_q, -1, 1)
    both(ev_q, 1, -1)
    both(ev_q, 1, 1)
    both(ev_q2, 0)
    both(ev_q, 2, -1)
    both(ev_q, 2, 1)
    both(ev_q2, -1)
    both(ev_q2, 1)
    both(ev_q2, 2)

    def norm_into(f, gain_ref):
        gain = gain_ref[...]
        for i in range(PAD // 16):
            rows = pl.ds(16 * i, 16)
            act[rows, :] = norm_rows(state[f, rows, :], gain).astype(BF)

    def project(f):
        norm_into(f, again_ref)

        for at in range(0, 3 * D, 256):
            packed[:, at:at + 256] = dot(act[...], trip_v[:, at:at + 256]).astype(BF)

    def attend():
        low = lax.broadcasted_iota(jnp.int32, (PAD, 128), 1) < 64
        bias = jnp.where(lax.broadcasted_iota(jnp.int32, (1, PAD), 1) < ROWS, 0.0, -1e30).astype(F32)

        for at in range(0, D, 128):
            q = packed[:, at:at + 128]
            k = packed[:, D + at:D + at + 128]
            v = packed[:, 2 * D + at:2 * D + at + 128]
            parts = []
            for keep in (low, ~low):
                scores = dot_t(jnp.where(keep, q * 0.125, 0.0).astype(BF), k) + bias
                shares = jnp.exp(scores - jnp.max(scores, axis=-1, keepdims=True))
                total = jnp.sum(shares, axis=-1, keepdims=True)
                parts.append(dot(shares.astype(BF), v) / total)
            ctx[:, at:at + 128] = jnp.where(low, parts[0], parts[1]).astype(BF)

    def join(f):
        for at in range(0, D, 256):
            state[f, :, at:at + 256] += dot(ctx[...], outw_v[:, at:at + 256])

    def feed(f):
        norm_into(f, dgain_ref)
        wide = dot(act[...], exp_v[:, 0:256])
        for at in range(0, FF, 256):
            hidden = gelu(wide).astype(BF)
            if at + 256 < FF:
                wide = dot(act[...], exp_v[:, at + 256:at + 512])
            state[f] += dot(hidden, red_v[at:at + 256, :])

    for copy in loads[:2]:
        copy.wait()

    todo = list(events)

    def pump(count):
        for _ in range(min(count, len(todo))):
            todo.pop(0)()

    for f in range(NF):
        @pl.when(seg == 0)
        def _():
            state[f, 192:PAD, :] = jnp.zeros((PAD - 192, D), F32)
            state[f, 0:ROWS, :] = frames_ref[f].astype(F32)
            project(f)

        pump(4)

        @pl.when(seg == 0)
        def _():
            attend()

        pump(3)

        @pl.when(seg == 0)
        def _():
            join(f)

        pump(2)
    pump(len(todo))
    for kind in range(2):
        for dp in range(4):
            for dq in range(4):
                sibling(kind, dp, dq, receive=True).wait_recv()
    for copy in loads[2:]:
        copy.wait()

    def relay(f):
        return pltpu.make_async_remote_copy(
            src_ref=outb.at[f], dst_ref=inb.at[f], send_sem=rel_send.at[f], recv_sem=rel_recv.at[f],
            device_id=((seg + 1) % 4, lane), device_id_type=MESH)

    @pl.when(seg == 2)
    def _():
        pooled[...] = jnp.zeros_like(pooled)

    @pl.when(seg < 3)
    def _():
        def step(f, carry):
            @pl.when(seg > 0)
            def _():
                relay(f).wait_recv()
                state[f] = inb[f].astype(F32)
                project(f)
                attend()
                join(f)

            feed(f)

            @pl.when(seg < 2)
            def _():
                outb[f] = state[f].astype(BF)
                relay(f).start()

            @pl.when(seg == 2)
            def _():
                gain = fgain_ref[...]
                total = jnp.zeros((16, D), F32)
                for i in range(PAD // 16):
                    rows = norm_rows(state[f, pl.ds(16 * i, 16), :], gain)
                    if 16 * i + 16 > ROWS:
                        keep = lax.broadcasted_iota(jnp.int32, (16, D), 0) < ROWS - 16 * i
                        rows = jnp.where(keep, rows, 0.0)
                    total = total + rows
                pooled[pl.ds(f, 1), :] = jnp.sum(total, axis=0, keepdims=True) * (1.0 / ROWS)

            return carry

        lax.fori_loop(0, NF, step, 0)

    def pool_copy(d):
        return pltpu.make_async_remote_copy(
            src_ref=pooled, dst_ref=pin.at[pl.ds(8 * (d + REACH), 8), :],
            send_sem=pool_send.at[d + REACH], recv_sem=pool_recv.at[d + REACH],
            device_id=((seg + 1) % 4, (lane - d + 32) % 32), device_id_type=MESH)

    def result_copy(section):
        return pltpu.make_async_remote_copy(
            src_ref=obuf.at[section], dst_ref=rbuf, send_sem=fin_send.at[section], recv_sem=fin_recv,
            device_id=(section, lane), device_id_type=MESH)

    @pl.when(seg == 2)
    def _():
        for d in range(-REACH, REACH + 1):
            pool_copy(d).start()

    @pl.when(seg == 3)
    def _():
        pin[8 * SLOTS:KEYS, :] = jnp.zeros((KEYS - 8 * SLOTS, D), F32)
        for d in range(-REACH, REACH + 1):
            pool_copy(d).wait_recv()
        again = again_ref[...]
        for i in range(KEYS // 16):
            rows = pl.ds(16 * i, 16)
            act[rows, :] = norm_rows(pin[rows, :], again).astype(BF)

        def chunk(n, carry):
            cols = pl.ds(pl.multiple_of(n * 512, 512), 512)
            packed[0:KEYS, cols] = dot(act[0:KEYS, :], trip_v[:, cols]).astype(BF)
            return carry

        lax.fori_loop(0, 6, chunk, 0)

        col = lax.broadcasted_iota(jnp.int32, (16, KEYS), 1)
        row = lax.broadcasted_iota(jnp.int32, (16, KEYS), 0)
        key_lane = (lane + (col >> 3) - REACH + 32) & 31
        key_at = key_lane * NF + (col & 7)
        own_at = lane * NF + jnp.minimum(row, NF - 1)
        key_shot = jnp.zeros((16, KEYS), jnp.int32)
        own_shot = jnp.zeros((16, KEYS), jnp.int32)
        end = 0
        for s in range(24):
            end = end + shot_ref[s]
            key_shot += (key_at >= end).astype(jnp.int32)
            own_shot += (own_at >= end).astype(jnp.int32)
        allowed = (key_shot == own_shot) & ((col & 7) < NF) & (col < 8 * SLOTS)
        low = lax.broadcasted_iota(jnp.int32, (16, 128), 1) < 64
        mine = 8 * REACH

        def pair(j, carry):
            at = pl.multiple_of(j * 128, 128)
            q = packed[mine:mine + 16, pl.ds(at, 128)]
            k = packed[0:KEYS, pl.ds(pl.multiple_of(at + D, 128), 128)]
            v = packed[0:KEYS, pl.ds(pl.multiple_of(at + 2 * D, 128), 128)]
            parts = []
            for keep in (low, ~low):
                scores = dot_t(jnp.where(keep, q * 0.125, 0.0).astype(BF), k)
                scores = jnp.where(allowed, scores, -1e30)
                shares = jnp.exp(scores - jnp.max(scores, axis=-1, keepdims=True))
                total = jnp.sum(shares, axis=-1, keepdims=True)
                high = shares.astype(BF)
                rest = (shares - high.astype(F32)).astype(BF)
                parts.append((dot(high, v) + dot(rest, v)) / total)
            ctx[0:16, pl.ds(at, 128)] = jnp.where(low, parts[0], parts[1]).astype(BF)
            return carry

        lax.fori_loop(0, 8, pair, 0)
        temporal = pin[mine:mine + 16, :] + dot(ctx[0:16, :], outw_v[...])
        state[0, 0:16, :] = temporal
        act[0:16, :] = norm_rows(temporal, dgain_ref[...]).astype(BF)

        def ff_chunk(n, carry):
            part = pl.ds(pl.multiple_of(n * 512, 512), 512)
            hidden = gelu(dot(act[0:16, :], exp_v[:, part])).astype(BF)
            state[0, 0:16, :] += dot(hidden, red_v[part, :])
            return carry

        lax.fori_loop(0, 8, ff_chunk, 0)
        for section in range(4):
            obuf[section] = state[0, 0:8, 256 * section:256 * section + 256]
        for section in range(3):
            result_copy(section).start()
        out_ref[...] = obuf[3, 0:NF, :]
        for section in range(3):
            result_copy(section).wait_send()

    @pl.when(seg == 2)
    def _():
        for d in range(-REACH, REACH + 1):
            pool_copy(d).wait_send()

    @pl.when(seg < 2)
    def _():
        for f in range(NF):
            relay(f).wait_send()

    for copy in sent:
        copy.wait_send()

    @pl.when(seg < 3)
    def _():
        result_copy(0).wait_recv()
        out_ref[...] = rbuf[0:NF, :]


def body(frames, triple_weight, output_weight, expand_weight, reduce_weight, attend_gain, dense_gain, final_gain, shot_lengths):
    vmem = pl.BlockSpec(memory_space=pltpu.VMEM)
    anywhere = pl.BlockSpec(memory_space=pl.ANY)
    dma = pltpu.SemaphoreType.DMA
    return pl.pallas_call(
        kernel,
        out_shape=jax.ShapeDtypeStruct((NF, 256), F32),
        in_specs=[vmem, anywhere, anywhere, anywhere, anywhere, vmem, vmem, vmem,
                  pl.BlockSpec(memory_space=pltpu.SMEM)],
        out_specs=vmem,
        scratch_shapes=[
            pltpu.VMEM((D, FF), BF), pltpu.VMEM((FF, D), BF), pltpu.VMEM((D, 3 * D), BF), pltpu.VMEM((D, D), BF),
            pltpu.VMEM((NF, PAD, D), F32), pltpu.VMEM((NF, PAD, D), BF), pltpu.VMEM((NF, PAD, D), BF),
            pltpu.VMEM((PAD, 3 * D), BF), pltpu.VMEM((PAD, D), BF), pltpu.VMEM((PAD, D), BF),
            pltpu.VMEM((8, D), F32), pltpu.VMEM((KEYS, D), F32), pltpu.VMEM((4, 8, 256), F32), pltpu.VMEM((8, 256), F32),
            dma((4,)), dma((2, 4, 4, 2)), dma((2, 4, 4, 2)), dma((2, 4, 4)), dma((2, 4, 4)),
            dma((NF,)), dma((NF,)), dma((SLOTS,)), dma((SLOTS,)), dma((3,)), dma(()),
        ],
        compiler_params=pltpu.CompilerParams(
            collective_id=0, has_side_effects=True, vmem_limit_bytes=60 * 1024 * 1024),
    )(frames, triple_weight, output_weight, expand_weight, reduce_weight, attend_gain, dense_gain,
      final_gain.reshape(1, D), shot_lengths)


def solution(mesh):
    return jax.shard_map(
        body,
        mesh=mesh,
        in_specs=(
            P("lane", None, None),
            P("segment", None, None),
            P("segment", None, None),
            P("segment", None, "lane"),
            P("segment", "lane", None),
            P("segment", None),
            P("segment", None),
            P(),
            P(),
        ),
        out_specs=P("lane", "segment"),
        check_vma=False,
    )
```

```python
import functools
import math

import jax
import jax.numpy as jnp
from jax import lax
from jax.experimental import pallas as pl
from jax.experimental.pallas import tpu as pltpu
from jax.sharding import PartitionSpec as P

HEADS = 16
ROWS = 197
PAD = 208
D = 1024
FF = 4096
NF = 3
REACH = 4
SLOTS = 2 * REACH + 1
KEYS = 80
MESH = pl.DeviceIdType.MESH
F32 = jnp.float32
BF = jnp.bfloat16


def dot(a, b):
    return lax.dot_general(a, b, (((1,), (0,)), ((), ())), preferred_element_type=F32)


def dot_t(a, b):
    return lax.dot_general(a, b, (((1,), (1,)), ((), ())), preferred_element_type=F32)


def gelu(x):
    return 0.5 * x * (1.0 + lax.erf(x * (1.0 / math.sqrt(2.0))))


def norm_rows(x, gain):
    average = jnp.mean(x, axis=-1, keepdims=True)
    centred = x - average
    spread = jnp.mean(centred * centred, axis=-1, keepdims=True)
    return centred * lax.rsqrt(spread + 1e-06) * gain


def kernel(
    frames_ref, triple_hbm, output_hbm, expand_hbm, reduce_hbm, again_ref, dgain_ref, fgain_ref, shot_ref,
    out_ref,
    exp_v, red_v, exp_h, red_h, trip_v, outw_v, state, inb, inp, outb, outy, packed, act, ctx, pooled, pin, obuf, rbuf,
    local_sem, send_sem, recv_sem, sib_send, sib_recv, hsend_sem, hrecv_sem, hsib_send, hsib_recv,
    rel_send, rel_recv, early_send, part_send, part_recv, shard_send, shard_recv,
    pool_send, pool_recv, fin_send, fin_recv,
):
    seg = lax.axis_index("segment")
    lane = lax.axis_index("lane")
    cx = lane // 8
    cz = (lane // 2) % 4
    core = lane % 2

    def lane_at(x, z, c):
        return ((x % 4) * 4 + (z % 4)) * 2 + c

    loads = [
        pltpu.make_async_copy(triple_hbm.at[0], trip_v, local_sem.at[0]),
        pltpu.make_async_copy(output_hbm.at[0], outw_v, local_sem.at[1]),
    ]
    for copy in loads:
        copy.start()

    peers = [
        (seg, lane_at(cx + 1, cz, core)), (seg, lane_at(cx + 3, cz, core)),
        (seg, lane_at(cx, cz + 1, core)), (seg, lane_at(cx, cz + 3, core)),
        (seg, lane_at(cx, cz, 1 - core)),
        ((seg + 1) % 4, lane), ((seg + 2) % 4, lane), ((seg + 3) % 4, lane),
    ]
    barrier = pltpu.get_barrier_semaphore()
    for peer in peers:
        pl.semaphore_signal(barrier, inc=1, device_id=peer, device_id_type=MESH)
    pl.semaphore_wait(barrier, len(peers))

    own_src = (expand_hbm.at[0], reduce_hbm.at[0])

    def pane(exp_ref, red_ref, kind, owner, half):
        if kind == 0:
            cols = pl.ds(pl.multiple_of(owner * 128, 128), 128)
            rows = pl.ds(0, D) if half is None else pl.ds(half * (D // 2), D // 2)
            return exp_ref.at[rows, cols]
        if half is None:
            return red_ref.at[pl.ds(pl.multiple_of(owner * 128, 128), 128), :]
        return red_ref.at[pl.ds(pl.multiple_of(owner * 128 + half * 64, 64), 64), :]

    def make_ring(exp_ref, red_ref, halved, ssem, rsem, bsend, brecv):
        def region(kind, dp, dq, c, half):
            x, z = (cx + dp + 4, cz + dq + 4) if kind == 0 else (cx + dq + 4, cz + dp + 4)
            owner = lane_at(x, z, 0) // 2 if halved else lane_at(x, z, c)
            return pane(exp_ref, red_ref, kind, owner, half)

        def neighbour(kind, along_p, sign):
            s = sign + 4
            if (kind == 0) == along_p:
                return (seg, lane_at(cx + s, cz, core))
            return (seg, lane_at(cx, cz + s, core))

        def source(kind, dp, dq, dst):
            return own_src[kind] if dp == 0 and dq == 0 and not halved else dst

        def hop(kind, dp, dq, half, along_p, sign):
            rp, rq = (dp - sign, dq) if along_p else (dp, dq - sign)
            h = half or 0
            dst = region(kind, dp, dq, core, half)
            return pltpu.make_async_remote_copy(
                src_ref=source(kind, dp, dq, dst), dst_ref=dst,
                send_sem=ssem.at[kind, rp % 4, rq % 4, h], recv_sem=rsem.at[kind, rp % 4, rq % 4, h],
                device_id=neighbour(kind, along_p, sign), device_id_type=MESH)

        def arrival(kind, rp, rq, half):
            h = half or 0
            dst = region(kind, rp, rq, core, half)
            return pltpu.make_async_remote_copy(
                src_ref=dst, dst_ref=dst,
                send_sem=ssem.at[kind, rp % 4, rq % 4, h], recv_sem=rsem.at[kind, rp % 4, rq % 4, h],
                device_id=neighbour(kind, True, 1), device_id_type=MESH)

        def sibling(kind, dp, dq, receive=False):
            dst = region(kind, dp, dq, 1 - core if receive else core, None)
            return pltpu.make_async_remote_copy(
                src_ref=dst if receive else source(kind, dp, dq, dst), dst_ref=dst,
                send_sem=bsend.at[kind, dp % 4, dq % 4], recv_sem=brecv.at[kind, dp % 4, dq % 4],
                device_id=(seg, lane_at(cx, cz, 1 - core)), device_id_type=MESH)

        sent = []

        def go(make, *args):
            make(*args).start()
            sent.append((make, args))

        def start():
            for kind in range(2):
                for sign in (1, -1):
                    go(hop, kind, 0, 0, None, True, sign)
            for kind in range(2):
                for sign in (1, -1):
                    go(hop, kind, 0, 0, None, False, sign)
                go(sibling, kind, 0, 0)

        def spread(kind, dp):
            for sign in (1, -1):
                go(hop, kind, dp, 0, None, False, sign)
            go(sibling, kind, dp, 0)

        def ev_p(kind, rp):
            arrival(kind, rp, 0, None).wait_recv()
            go(hop, kind, rp, 0, 0 if rp < 0 else 1, True, -rp)
            spread(kind, rp)

        def ev_p2(kind):
            arrival(kind, 2, 0, 0).wait_recv()
            arrival(kind, 2, 0, 1).wait_recv()
            spread(kind, 2)

        def ev_q(kind, rp, rq):
            arrival(kind, rp, rq, None).wait_recv()
            go(hop, kind, rp, rq, 0 if rq < 0 else 1, False, -rq)
            go(sibling, kind, rp, rq)

        def ev_q2(kind, rp):
            arrival(kind, rp, 2, 0).wait_recv()
            arrival(kind, rp, 2, 1).wait_recv()
            go(sibling, kind, rp, 2)

        events = []

        def both(fn, *args):
            for kind in range(2):
                events.append(functools.partial(fn, kind, *args))

        both(ev_p, -1)
        both(ev_p, 1)
        both(ev_q, 0, -1)
        both(ev_q, 0, 1)
        both(ev_p2)
        both(ev_q, -1, -1)
        both(ev_q, -1, 1)
        both(ev_q, 1, -1)
        both(ev_q, 1, 1)
        both(ev_q2, 0)
        both(ev_q, 2, -1)
        both(ev_q, 2, 1)
        both(ev_q2, -1)
        both(ev_q2, 1)
        both(ev_q2, 2)

        def pump(count):
            for _ in range(min(count, len(events))):
                events.pop(0)()

        def from_sibling():
            for kind in range(2):
                for dp in range(4):
                    for dq in range(4):
                        sibling(kind, dp, dq, True).wait_recv()

        def drain():
            for make, args in sent:
                make(*args).wait_send()

        return start, pump, from_sibling, drain

    full_start, full_pump, full_sibling, full_drain = make_ring(
        exp_v, red_v, False, send_sem, recv_sem, sib_send, sib_recv)
    half_start, half_pump, half_sibling, half_drain = make_ring(
        exp_h, red_h, True, hsend_sem, hrecv_sem, hsib_send, hsib_recv)

    halves = (seg == 0) | (seg == 3)
    active = ((seg == 0) & (core == 0)) | ((seg == 3) & (core == 1))

    def shard(kind):
        return pltpu.make_async_remote_copy(
            src_ref=own_src[kind], dst_ref=pane(exp_h, red_h, kind, lane // 2, None),
            send_sem=shard_send.at[kind], recv_sem=shard_recv.at[kind],
            device_id=((seg + 3) % 4, lane), device_id_type=MESH)

    def own_load(kind, exp_ref, red_ref, owner):
        return pltpu.make_async_copy(own_src[kind], pane(exp_ref, red_ref, kind, owner, None), local_sem.at[2 + kind])

    @pl.when((seg == 0) & (core == 1))
    def _():
        for kind in range(2):
            shard(kind).start()

    @pl.when((seg == 0) & (core == 0))
    def _():
        for kind in range(2):
            own_load(kind, exp_h, red_h, lane // 2).start()
        for kind in range(2):
            own_load(kind, exp_h, red_h, lane // 2).wait()

    @pl.when((seg == 3) & (core == 1))
    def _():
        for kind in range(2):
            shard(kind).wait_recv()

    @pl.when(active)
    def _():
        half_start()

    def norm_into(f, gain_ref):
        gain = gain_ref[...]
        for i in range(PAD // 16):
            rows = pl.ds(16 * i, 16)
            act[rows, :] = norm_rows(state[f, rows, :], gain).astype(BF)

    def project(f):
        norm_into(f, again_ref)

        for at in range(0, 3 * D, 256):
            packed[:, at:at + 256] = dot(act[...], trip_v[:, at:at + 256]).astype(BF)

    def attend():
        low = lax.broadcasted_iota(jnp.int32, (PAD, 128), 1) < 64
        bias = jnp.where(lax.broadcasted_iota(jnp.int32, (1, PAD), 1) < ROWS, 0.0, -1e30).astype(F32)

        for at in range(0, D, 128):
            q = packed[:, at:at + 128]
            k = packed[:, D + at:D + at + 128]
            v = packed[:, 2 * D + at:2 * D + at + 128]
            parts = []
            for keep in (low, ~low):
                scores = dot_t(jnp.where(keep, q * 0.125, 0.0).astype(BF), k) + bias
                shares = jnp.exp(scores - jnp.max(scores, axis=-1, keepdims=True))
                total = jnp.sum(shares, axis=-1, keepdims=True)
                parts.append(dot(shares.astype(BF), v) / total)
            ctx[:, at:at + 128] = jnp.where(low, parts[0], parts[1]).astype(BF)

    def join(f):
        for at in range(0, D, 256):
            state[f, :, at:at + 256] += dot(ctx[...], outw_v[:, at:at + 256])

    def feed(f, exp_ref, red_ref, depth):
        wide = dot(act[...], exp_ref[:, 0:256])
        for at in range(0, depth, 256):
            hidden = gelu(wide).astype(BF)
            if at + 256 < depth:
                wide = dot(act[...], exp_ref[:, at + 256:at + 512])
            state[f] += dot(hidden, red_ref[at:at + 256, :])

    for copy in loads[:2]:
        copy.wait()

    def relay(f):
        return pltpu.make_async_remote_copy(
            src_ref=outb.at[f], dst_ref=inb.at[f], send_sem=rel_send.at[f], recv_sem=rel_recv.at[f],
            device_id=((seg + 1) % 4, lane), device_id_type=MESH)

    def early(f):
        return pltpu.make_async_remote_copy(
            src_ref=outy.at[f], dst_ref=inb.at[f], send_sem=early_send.at[f], recv_sem=rel_recv.at[f],
            device_id=((seg + 3) % 4, lane), device_id_type=MESH)

    def partial(f):
        return pltpu.make_async_remote_copy(
            src_ref=outb.at[f], dst_ref=inp.at[f], send_sem=part_send.at[f], recv_sem=part_recv.at[f],
            device_id=((seg + 2) % 4, lane), device_id_type=MESH)

    @pl.when(halves)
    def _():
        for f in range(NF):
            @pl.when(seg == 0)
            def _():
                state[f, 192:PAD, :] = jnp.zeros((PAD - 192, D), F32)
                state[f, 0:ROWS, :] = frames_ref[f].astype(F32)
                project(f)

            @pl.when(active)
            def _():
                half_pump(4)

            @pl.when(seg == 0)
            def _():
                attend()

            @pl.when(active)
            def _():
                half_pump(4)

            @pl.when(seg == 0)
            def _():
                join(f)
                norm_into(f, dgain_ref)
                outy[f] = act[...]
                early(f).start()

            @pl.when(active)
            def _():
                half_pump(2)

        @pl.when(active)
        def _():
            half_pump(1000)

        @pl.when(~active)
        def _():
            half_sibling()

        def step(f, carry):
            @pl.when(seg == 3)
            def _():
                early(f).wait_recv()
                act[...] = inb[f]
                state[f] = jnp.zeros((PAD, D), F32)

            @pl.when(seg == 0)
            def _():
                act[...] = outy[f]

            feed(f, exp_h, red_h, FF // 2)
            outb[f] = state[f].astype(BF)

            @pl.when(seg == 0)
            def _():
                relay(f).start()

            @pl.when(seg == 3)
            def _():
                partial(f).start()

            return carry

        lax.fori_loop(0, NF, step, 0)

    @pl.when(seg > 0)
    def _():
        full_start()
        for kind in range(2):
            own_load(kind, exp_v, red_v, lane).start()
        full_pump(1000)
        full_sibling()
        for kind in range(2):
            own_load(kind, exp_v, red_v, lane).wait()

    @pl.when(seg == 2)
    def _():
        pooled[...] = jnp.zeros_like(pooled)

    @pl.when((seg == 1) | (seg == 2))
    def _():
        def step(f, carry):
            relay(f).wait_recv()

            @pl.when(seg == 2)
            def _():
                state[f] = inb[f].astype(F32)

            @pl.when(seg == 1)
            def _():
                partial(f).wait_recv()
                state[f] = inb[f].astype(F32) + inp[f].astype(F32)

            project(f)
            attend()
            join(f)
            norm_into(f, dgain_ref)
            feed(f, exp_v, red_v, FF)

            @pl.when(seg == 1)
            def _():
                outb[f] = state[f].astype(BF)
                relay(f).start()

            @pl.when(seg == 2)
            def _():
                gain = fgain_ref[...]
                total = jnp.zeros((16, D), F32)
                for i in range(PAD // 16):
                    rows = norm_rows(state[f, pl.ds(16 * i, 16), :], gain)
                    if 16 * i + 16 > ROWS:
                        keep = lax.broadcasted_iota(jnp.int32, (16, D), 0) < ROWS - 16 * i
                        rows = jnp.where(keep, rows, 0.0)
                    total = total + rows
                pooled[pl.ds(f, 1), :] = jnp.sum(total, axis=0, keepdims=True) * (1.0 / ROWS)

            return carry

        lax.fori_loop(0, NF, step, 0)

    def pool_copy(d):
        return pltpu.make_async_remote_copy(
            src_ref=pooled, dst_ref=pin.at[pl.ds(8 * (d + REACH), 8), :],
            send_sem=pool_send.at[d + REACH], recv_sem=pool_recv.at[d + REACH],
            device_id=((seg + 1) % 4, (lane - d + 32) % 32), device_id_type=MESH)

    def result_copy(section):
        return pltpu.make_async_remote_copy(
            src_ref=obuf.at[section], dst_ref=rbuf, send_sem=fin_send.at[section], recv_sem=fin_recv,
            device_id=(section, lane), device_id_type=MESH)

    @pl.when(seg == 2)
    def _():
        for d in range(-REACH, REACH + 1):
            pool_copy(d).start()

    @pl.when(seg == 3)
    def _():
        pin[8 * SLOTS:KEYS, :] = jnp.zeros((KEYS - 8 * SLOTS, D), F32)
        for d in range(-REACH, REACH + 1):
            pool_copy(d).wait_recv()
        again = again_ref[...]
        for i in range(KEYS // 16):
            rows = pl.ds(16 * i, 16)
            act[rows, :] = norm_rows(pin[rows, :], again).astype(BF)

        for at in range(0, 3 * D, 256):
            packed[0:KEYS, at:at + 256] = dot(act[0:KEYS, :], trip_v[:, at:at + 256]).astype(BF)

        col = lax.broadcasted_iota(jnp.int32, (16, KEYS), 1)
        row = lax.broadcasted_iota(jnp.int32, (16, KEYS), 0)
        key_lane = (lane + (col >> 3) - REACH + 32) & 31
        key_at = key_lane * NF + (col & 7)
        own_at = lane * NF + jnp.minimum(row, NF - 1)
        key_shot = jnp.zeros((16, KEYS), jnp.int32)
        own_shot = jnp.zeros((16, KEYS), jnp.int32)
        end = 0
        for s in range(24):
            end = end + shot_ref[s]
            key_shot += (key_at >= end).astype(jnp.int32)
            own_shot += (own_at >= end).astype(jnp.int32)
        allowed = (key_shot == own_shot) & ((col & 7) < NF) & (col < 8 * SLOTS)
        low = lax.broadcasted_iota(jnp.int32, (16, 128), 1) < 64
        mine = 8 * REACH

        for at in range(0, D, 128):
            q = packed[mine:mine + 16, at:at + 128]
            k = packed[0:KEYS, D + at:D + at + 128]
            v = packed[0:KEYS, 2 * D + at:2 * D + at + 128]
            parts = []
            for keep in (low, ~low):
                scores = dot_t(jnp.where(keep, q * 0.125, 0.0).astype(BF), k)
                scores = jnp.where(allowed, scores, -1e30)
                shares = jnp.exp(scores - jnp.max(scores, axis=-1, keepdims=True))
                total = jnp.sum(shares, axis=-1, keepdims=True)
                high = shares.astype(BF)
                rest = (shares - high.astype(F32)).astype(BF)
                parts.append((dot(high, v) + dot(rest, v)) / total)
            ctx[0:16, at:at + 128] = jnp.where(low, parts[0], parts[1]).astype(BF)

        temporal = pin[mine:mine + 16, :] + dot(ctx[0:16, :], outw_v[...])
        act[0:16, :] = norm_rows(temporal, dgain_ref[...]).astype(BF)

        wide = dot(act[0:16, :], exp_v[:, 0:256])
        for at in range(0, FF, 256):
            hidden = gelu(wide).astype(BF)
            if at + 256 < FF:
                wide = dot(act[0:16, :], exp_v[:, at + 256:at + 512])
            temporal = temporal + dot(hidden, red_v[at:at + 256, :])

        for section in range(4):
            obuf[section] = temporal[0:8, 256 * section:256 * section + 256]
        for section in range(3):
            result_copy(section).start()
        out_ref[...] = obuf[3, 0:NF, :]
        for section in range(3):
            result_copy(section).wait_send()

    @pl.when(seg == 2)
    def _():
        for d in range(-REACH, REACH + 1):
            pool_copy(d).wait_send()

    @pl.when(seg < 2)
    def _():
        for f in range(NF):
            relay(f).wait_send()

    @pl.when(seg == 0)
    def _():
        for f in range(NF):
            early(f).wait_send()

    @pl.when(seg == 3)
    def _():
        for f in range(NF):
            partial(f).wait_send()

    @pl.when((seg == 0) & (core == 1))
    def _():
        for kind in range(2):
            shard(kind).wait_send()

    @pl.when(active)
    def _():
        half_drain()

    @pl.when(seg > 0)
    def _():
        full_drain()

    @pl.when(seg < 3)
    def _():
        result_copy(0).wait_recv()
        out_ref[...] = rbuf[0:NF, :]


def body(frames, triple_weight, output_weight, expand_weight, reduce_weight, attend_gain, dense_gain, final_gain, shot_lengths):
    vmem = pl.BlockSpec(memory_space=pltpu.VMEM)
    anywhere = pl.BlockSpec(memory_space=pl.ANY)
    dma = pltpu.SemaphoreType.DMA
    return pl.pallas_call(
        kernel,
        out_shape=jax.ShapeDtypeStruct((NF, 256), F32),
        in_specs=[vmem, anywhere, anywhere, anywhere, anywhere, vmem, vmem, vmem,
                  pl.BlockSpec(memory_space=pltpu.SMEM)],
        out_specs=vmem,
        scratch_shapes=[
            pltpu.VMEM((D, FF), BF), pltpu.VMEM((FF, D), BF),
            pltpu.VMEM((D, FF // 2), BF), pltpu.VMEM((FF // 2, D), BF), pltpu.VMEM((D, 3 * D), BF), pltpu.VMEM((D, D), BF),
            pltpu.VMEM((NF, PAD, D), F32), pltpu.VMEM((NF, PAD, D), BF), pltpu.VMEM((NF, PAD, D), BF),
            pltpu.VMEM((NF, PAD, D), BF), pltpu.VMEM((NF, PAD, D), BF),
            pltpu.VMEM((PAD, 3 * D), BF), pltpu.VMEM((PAD, D), BF), pltpu.VMEM((PAD, D), BF),
            pltpu.VMEM((8, D), F32), pltpu.VMEM((KEYS, D), F32), pltpu.VMEM((4, 8, 256), F32), pltpu.VMEM((8, 256), F32),
            dma((4,)), dma((2, 4, 4, 2)), dma((2, 4, 4, 2)), dma((2, 4, 4)), dma((2, 4, 4)),
            dma((2, 4, 4, 2)), dma((2, 4, 4, 2)), dma((2, 4, 4)), dma((2, 4, 4)),
            dma((NF,)), dma((NF,)), dma((NF,)), dma((NF,)), dma((NF,)), dma((2,)), dma((2,)),
            dma((SLOTS,)), dma((SLOTS,)), dma((3,)), dma(()),
        ],
        compiler_params=pltpu.CompilerParams(
            collective_id=0, has_side_effects=True, vmem_limit_bytes=60 * 1024 * 1024),
    )(frames, triple_weight, output_weight, expand_weight, reduce_weight, attend_gain, dense_gain,
      final_gain.reshape(1, D), shot_lengths)


def solution(mesh):
    return jax.shard_map(
        body,
        mesh=mesh,
        in_specs=(
            P("lane", None, None),
            P("segment", None, None),
            P("segment", None, None),
            P("segment", None, "lane"),
            P("segment", "lane", None),
            P("segment", None),
            P("segment", None),
            P(),
            P(),
        ),
        out_specs=P("lane", "segment"),
        check_vma=False,
    )
```

```python
import functools
import math

import jax
import jax.numpy as jnp
from jax import lax
from jax.experimental import pallas as pl
from jax.experimental.pallas import tpu as pltpu
from jax.sharding import PartitionSpec as P

HEADS = 16
ROWS = 197
PAD = 208
SENT = 200
D = 1024
FF = 4096
NF = 3
REACH = 4
SLOTS = 2 * REACH + 1
KEYS = 32
MINE = NF * REACH
MESH = pl.DeviceIdType.MESH
F32 = jnp.float32
BF = jnp.bfloat16


def dot(a, b):
    return lax.dot_general(a, b, (((1,), (0,)), ((), ())), preferred_element_type=F32)


def dot_t(a, b):
    return lax.dot_general(a, b, (((1,), (1,)), ((), ())), preferred_element_type=F32)


def gelu(x):
    return 0.5 * x * (1.0 + lax.erf(x * (1.0 / math.sqrt(2.0))))


def norm_rows(x, gain):
    average = jnp.mean(x, axis=-1, keepdims=True)
    centred = x - average
    spread = jnp.mean(centred * centred, axis=-1, keepdims=True)
    return centred * lax.rsqrt(spread + 1e-06) * gain


def kernel(
    frames_ref, triple_hbm, output_hbm, expand_hbm, reduce_hbm, again_ref, dgain_ref, fgain_ref, shot_ref,
    out_ref,
    exp_v, red_v, exp_h, red_h, trip_v, outw_v, state, inb, inp, outb, outy, packed, act, ctx, pooled, pin, obuf, rbuf,
    local_sem, send_sem, recv_sem, sib_send, sib_recv, hsend_sem, hrecv_sem, hsib_send, hsib_recv,
    rel_send, rel_recv, early_send, part_send, part_recv, shard_send, shard_recv,
    pool_send, pool_recv, fin_send, fin_recv,
):
    seg = lax.axis_index("segment")
    lane = lax.axis_index("lane")
    cx = lane // 8
    cz = (lane // 2) % 4
    core = lane % 2

    def lane_at(x, z, c):
        return ((x % 4) * 4 + (z % 4)) * 2 + c

    loads = [
        pltpu.make_async_copy(triple_hbm.at[0], trip_v, local_sem.at[0]),
        pltpu.make_async_copy(output_hbm.at[0], outw_v, local_sem.at[1]),
    ]
    for copy in loads:
        copy.start()

    for f in range(NF):
        inb[f, 192:PAD, :] = jnp.zeros((PAD - 192, D), BF)
        inp[f, 192:PAD, :] = jnp.zeros((PAD - 192, D), BF)

    peers = [
        (seg, lane_at(cx + 1, cz, core)), (seg, lane_at(cx + 3, cz, core)),
        (seg, lane_at(cx, cz + 1, core)), (seg, lane_at(cx, cz + 3, core)),
        (seg, lane_at(cx, cz, 1 - core)),
        ((seg + 1) % 4, lane), ((seg + 2) % 4, lane), ((seg + 3) % 4, lane),
    ]
    barrier = pltpu.get_barrier_semaphore()
    for peer in peers:
        pl.semaphore_signal(barrier, inc=1, device_id=peer, device_id_type=MESH)
    pl.semaphore_wait(barrier, len(peers))

    own_src = (expand_hbm.at[0], reduce_hbm.at[0])

    def pane(exp_ref, red_ref, kind, owner, half):
        if kind == 0:
            cols = pl.ds(pl.multiple_of(owner * 128, 128), 128)
            rows = pl.ds(0, D) if half is None else pl.ds(half * (D // 2), D // 2)
            return exp_ref.at[rows, cols]
        if half is None:
            return red_ref.at[pl.ds(pl.multiple_of(owner * 128, 128), 128), :]
        return red_ref.at[pl.ds(pl.multiple_of(owner * 128 + half * 64, 64), 64), :]

    def make_ring(exp_ref, red_ref, halved, ssem, rsem, bsend, brecv):
        def region(kind, dp, dq, c, half):
            x, z = (cx + dp + 4, cz + dq + 4) if kind == 0 else (cx + dq + 4, cz + dp + 4)
            owner = lane_at(x, z, 0) // 2 if halved else lane_at(x, z, c)
            return pane(exp_ref, red_ref, kind, owner, half)

        def neighbour(kind, along_p, sign):
            s = sign + 4
            if (kind == 0) == along_p:
                return (seg, lane_at(cx + s, cz, core))
            return (seg, lane_at(cx, cz + s, core))

        def source(kind, dp, dq, dst):
            return own_src[kind] if dp == 0 and dq == 0 and not halved else dst

        def hop(kind, dp, dq, half, along_p, sign):
            rp, rq = (dp - sign, dq) if along_p else (dp, dq - sign)
            h = half or 0
            dst = region(kind, dp, dq, core, half)
            return pltpu.make_async_remote_copy(
                src_ref=source(kind, dp, dq, dst), dst_ref=dst,
                send_sem=ssem.at[kind, rp % 4, rq % 4, h], recv_sem=rsem.at[kind, rp % 4, rq % 4, h],
                device_id=neighbour(kind, along_p, sign), device_id_type=MESH)

        def arrival(kind, rp, rq, half):
            h = half or 0
            dst = region(kind, rp, rq, core, half)
            return pltpu.make_async_remote_copy(
                src_ref=dst, dst_ref=dst,
                send_sem=ssem.at[kind, rp % 4, rq % 4, h], recv_sem=rsem.at[kind, rp % 4, rq % 4, h],
                device_id=neighbour(kind, True, 1), device_id_type=MESH)

        def sibling(kind, dp, dq, receive=False):
            dst = region(kind, dp, dq, 1 - core if receive else core, None)
            return pltpu.make_async_remote_copy(
                src_ref=dst if receive else source(kind, dp, dq, dst), dst_ref=dst,
                send_sem=bsend.at[kind, dp % 4, dq % 4], recv_sem=brecv.at[kind, dp % 4, dq % 4],
                device_id=(seg, lane_at(cx, cz, 1 - core)), device_id_type=MESH)

        sent = []

        def go(make, *args):
            make(*args).start()
            sent.append((make, args))

        def start(ready=None):
            for kind in range(2):
                if ready is not None:
                    ready(kind)
                for sign in (1, -1):
                    go(hop, kind, 0, 0, None, True, sign)
            for kind in range(2):
                for sign in (1, -1):
                    go(hop, kind, 0, 0, None, False, sign)
                go(sibling, kind, 0, 0)

        def spread(kind, dp):
            for sign in (1, -1):
                go(hop, kind, dp, 0, None, False, sign)
            go(sibling, kind, dp, 0)

        def ev_p(kind, rp):
            arrival(kind, rp, 0, None).wait_recv()
            go(hop, kind, rp, 0, 0 if rp < 0 else 1, True, -rp)
            spread(kind, rp)

        def ev_p2(kind):
            arrival(kind, 2, 0, 0).wait_recv()
            arrival(kind, 2, 0, 1).wait_recv()
            spread(kind, 2)

        def ev_q(kind, rp, rq):
            arrival(kind, rp, rq, None).wait_recv()
            go(hop, kind, rp, rq, 0 if rq < 0 else 1, False, -rq)
            go(sibling, kind, rp, rq)

        def ev_q2(kind, rp):
            arrival(kind, rp, 2, 0).wait_recv()
            arrival(kind, rp, 2, 1).wait_recv()
            go(sibling, kind, rp, 2)

        events = []

        def both(fn, *args):
            for kind in range(2):
                events.append(functools.partial(fn, kind, *args))

        both(ev_p, -1)
        both(ev_p, 1)
        both(ev_q, 0, -1)
        both(ev_q, 0, 1)
        both(ev_p2)
        both(ev_q, -1, -1)
        both(ev_q, -1, 1)
        both(ev_q, 1, -1)
        both(ev_q, 1, 1)
        both(ev_q2, 0)
        both(ev_q, 2, -1)
        both(ev_q, 2, 1)
        both(ev_q2, -1)
        both(ev_q2, 1)
        both(ev_q2, 2)

        def pump(count):
            for _ in range(min(count, len(events))):
                events.pop(0)()

        def from_sibling():
            for kind in range(2):
                for dp in range(4):
                    for dq in range(4):
                        sibling(kind, dp, dq, True).wait_recv()

        def drain():
            for make, args in sent:
                make(*args).wait_send()

        return start, pump, from_sibling, drain

    full_start, full_pump, full_sibling, full_drain = make_ring(
        exp_v, red_v, False, send_sem, recv_sem, sib_send, sib_recv)
    half_start, half_pump, half_sibling, half_drain = make_ring(
        exp_h, red_h, True, hsend_sem, hrecv_sem, hsib_send, hsib_recv)

    halves = (seg == 0) | (seg == 3)
    active = ((seg == 0) & (core == 0)) | ((seg == 3) & (core == 1))

    def shard(kind):
        return pltpu.make_async_remote_copy(
            src_ref=own_src[kind], dst_ref=pane(exp_h, red_h, kind, lane // 2, None),
            send_sem=shard_send.at[kind], recv_sem=shard_recv.at[kind],
            device_id=((seg + 3) % 4, lane), device_id_type=MESH)

    def own_load(kind, exp_ref, red_ref, owner):
        return pltpu.make_async_copy(own_src[kind], pane(exp_ref, red_ref, kind, owner, None), local_sem.at[2 + kind])

    @pl.when((seg == 0) & (core == 1))
    def _():
        for kind in range(2):
            shard(kind).start()

    @pl.when((seg == 0) & (core == 0))
    def _():
        for kind in range(2):
            own_load(kind, exp_h, red_h, lane // 2).start()

    def ready(kind):
        @pl.when(seg == 0)
        def _():
            own_load(kind, exp_h, red_h, lane // 2).wait()

        @pl.when(seg == 3)
        def _():
            shard(kind).wait_recv()

    @pl.when(active)
    def _():
        half_start(ready)

    def norm_into(f, gain_ref):
        gain = gain_ref[...]
        for i in range(PAD // 16):
            rows = pl.ds(16 * i, 16)
            act[rows, :] = norm_rows(state[f, rows, :], gain).astype(BF)

    def project(f):
        norm_into(f, again_ref)

        for at in range(0, 3 * D, 256):
            packed[:, at:at + 256] = dot(act[...], trip_v[:, at:at + 256]).astype(BF)

    def attend():
        low = lax.broadcasted_iota(jnp.int32, (PAD, 128), 1) < 64
        bias = jnp.where(lax.broadcasted_iota(jnp.int32, (1, PAD), 1) < ROWS, 0.0, -1e30).astype(F32)

        for at in range(0, D, 128):
            q = packed[:, at:at + 128]
            k = packed[:, D + at:D + at + 128]
            v = packed[:, 2 * D + at:2 * D + at + 128]
            parts = []
            for keep in (low, ~low):
                scores = dot_t(jnp.where(keep, q * 0.125, 0.0).astype(BF), k) + bias
                shares = jnp.exp(scores - jnp.max(scores, axis=-1, keepdims=True))
                total = jnp.sum(shares, axis=-1, keepdims=True)
                parts.append(dot(shares.astype(BF), v) / total)
            ctx[:, at:at + 128] = jnp.where(low, parts[0], parts[1]).astype(BF)

    def join(f):
        for at in range(0, D, 256):
            state[f, :, at:at + 256] += dot(ctx[...], outw_v[:, at:at + 256])

    def feed(f, exp_ref, red_ref, depth):
        wide = dot(act[...], exp_ref[:, 0:256])
        for at in range(0, depth, 256):
            hidden = gelu(wide).astype(BF)
            if at + 256 < depth:
                wide = dot(act[...], exp_ref[:, at + 256:at + 512])
            state[f] += dot(hidden, red_ref[at:at + 256, :])

    for copy in loads[:2]:
        copy.wait()

    def relay(f):
        return pltpu.make_async_remote_copy(
            src_ref=outb.at[f, 0:SENT, :], dst_ref=inb.at[f, 0:SENT, :], send_sem=rel_send.at[f], recv_sem=rel_recv.at[f],
            device_id=((seg + 1) % 4, lane), device_id_type=MESH)

    def early(f):
        return pltpu.make_async_remote_copy(
            src_ref=outy.at[f, 0:SENT, :], dst_ref=inb.at[f, 0:SENT, :], send_sem=early_send.at[f], recv_sem=rel_recv.at[f],
            device_id=((seg + 3) % 4, lane), device_id_type=MESH)

    def partial(f):
        return pltpu.make_async_remote_copy(
            src_ref=outb.at[f, 0:SENT, :], dst_ref=inp.at[f, 0:SENT, :], send_sem=part_send.at[f], recv_sem=part_recv.at[f],
            device_id=((seg + 2) % 4, lane), device_id_type=MESH)

    @pl.when(halves)
    def _():
        for f in range(NF):
            @pl.when(seg == 0)
            def _():
                state[f, 192:PAD, :] = jnp.zeros((PAD - 192, D), F32)
                state[f, 0:ROWS, :] = frames_ref[f].astype(F32)
                project(f)

            @pl.when(active)
            def _():
                half_pump(4)

            @pl.when(seg == 0)
            def _():
                attend()

            @pl.when(active)
            def _():
                half_pump(4)

            @pl.when(seg == 0)
            def _():
                join(f)
                norm_into(f, dgain_ref)
                outy[f] = act[...]
                early(f).start()

            @pl.when(active)
            def _():
                half_pump(2)

        @pl.when(active)
        def _():
            half_pump(1000)

        @pl.when(~active)
        def _():
            half_sibling()

        def step(f, carry):
            @pl.when(seg == 3)
            def _():
                early(f).wait_recv()
                act[...] = inb[f]
                state[f] = jnp.zeros((PAD, D), F32)

            @pl.when(seg == 0)
            def _():
                act[...] = outy[f]

            feed(f, exp_h, red_h, FF // 2)
            outb[f] = state[f].astype(BF)

            @pl.when(seg == 0)
            def _():
                relay(f).start()

            @pl.when(seg == 3)
            def _():
                partial(f).start()

            return carry

        lax.fori_loop(0, NF, step, 0)

    @pl.when(seg > 0)
    def _():
        full_start()
        for kind in range(2):
            own_load(kind, exp_v, red_v, lane).start()
        full_pump(1000)

    def gathered():
        full_sibling()
        for kind in range(2):
            own_load(kind, exp_v, red_v, lane).wait()

    def pool_copy(f, d):
        return pltpu.make_async_remote_copy(
            src_ref=pooled.at[f], dst_ref=pin.at[d + REACH, f],
            send_sem=pool_send.at[f, d + REACH], recv_sem=pool_recv.at[f, d + REACH],
            device_id=((seg + 1) % 4, (lane - d + 32) % 32), device_id_type=MESH)

    @pl.when((seg == 1) | (seg == 2))
    def _():
        def step(f, carry):
            relay(f).wait_recv()

            @pl.when(seg == 2)
            def _():
                state[f] = inb[f].astype(F32)

            @pl.when(seg == 1)
            def _():
                partial(f).wait_recv()
                state[f] = inb[f].astype(F32) + inp[f].astype(F32)

            project(f)
            attend()
            join(f)
            norm_into(f, dgain_ref)

            @pl.when(f == 0)
            def _():
                gathered()

            feed(f, exp_v, red_v, FF)

            @pl.when(seg == 1)
            def _():
                outb[f] = state[f].astype(BF)
                relay(f).start()

            @pl.when(seg == 2)
            def _():
                gain = fgain_ref[...]
                total = jnp.zeros((16, D), F32)
                for i in range(PAD // 16):
                    rows = norm_rows(state[f, pl.ds(16 * i, 16), :], gain)
                    if 16 * i + 16 > ROWS:
                        keep = lax.broadcasted_iota(jnp.int32, (16, D), 0) < ROWS - 16 * i
                        rows = jnp.where(keep, rows, 0.0)
                    total = total + rows
                total = jnp.sum(total, axis=0, keepdims=True) * (1.0 / ROWS)
                for j in range(8):
                    pooled[f, j:j + 1, :] = total[:, 128 * j:128 * j + 128]
                for d in range(-REACH, REACH + 1):
                    pool_copy(f, d).start()

            return carry

        lax.fori_loop(0, NF, step, 0)

    def result_copy(section):
        return pltpu.make_async_remote_copy(
            src_ref=obuf.at[section], dst_ref=rbuf, send_sem=fin_send.at[section], recv_sem=fin_recv,
            device_id=(section, lane), device_id_type=MESH)

    @pl.when(seg == 3)
    def _():
        gathered()
        state[0, 24:KEYS, :] = jnp.zeros((KEYS - 24, D), F32)
        for f in range(NF):
            for d in range(-REACH, REACH + 1):
                pool_copy(f, d).wait_recv()
                row = NF * (d + REACH) + f
                for j in range(8):
                    state[0, row:row + 1, 128 * j:128 * j + 128] = pin[d + REACH, f, j:j + 1, :]
        again = again_ref[...]
        for i in range(KEYS // 16):
            rows = pl.ds(16 * i, 16)
            act[rows, :] = norm_rows(state[0, rows, :], again).astype(BF)

        for at in range(0, 3 * D, 256):
            packed[0:KEYS, at:at + 256] = dot(act[0:KEYS, :], trip_v[:, at:at + 256]).astype(BF)

        col = lax.broadcasted_iota(jnp.int32, (16, KEYS), 1)
        row = lax.broadcasted_iota(jnp.int32, (16, KEYS), 0)
        key_at = (lane - REACH) * NF + col
        key_at = jnp.where(key_at < 0, key_at + 32 * NF, key_at)
        key_at = jnp.where(key_at >= 32 * NF, key_at - 32 * NF, key_at)
        own_at = lane * NF + jnp.clip(row - MINE, 0, NF - 1)
        key_shot = jnp.zeros((16, KEYS), jnp.int32)
        own_shot = jnp.zeros((16, KEYS), jnp.int32)
        end = 0
        for s in range(24):
            end = end + shot_ref[s]
            key_shot += (key_at >= end).astype(jnp.int32)
            own_shot += (own_at >= end).astype(jnp.int32)
        allowed = (key_shot == own_shot) & (col < NF * SLOTS)
        low = lax.broadcasted_iota(jnp.int32, (16, 128), 1) < 64

        for at in range(0, D, 128):
            q = packed[0:16, at:at + 128]
            k = packed[0:KEYS, D + at:D + at + 128]
            v = packed[0:KEYS, 2 * D + at:2 * D + at + 128]
            parts = []
            for keep in (low, ~low):
                scores = dot_t(jnp.where(keep, q * 0.125, 0.0).astype(BF), k)
                scores = jnp.where(allowed, scores, -1e30)
                shares = jnp.exp(scores - jnp.max(scores, axis=-1, keepdims=True))
                total = jnp.sum(shares, axis=-1, keepdims=True)
                high = shares.astype(BF)
                rest = (shares - high.astype(F32)).astype(BF)
                parts.append((dot(high, v) + dot(rest, v)) / total)
            ctx[0:16, at:at + 128] = jnp.where(low, parts[0], parts[1]).astype(BF)

        temporal = state[0, 0:16, :] + dot(ctx[0:16, :], outw_v[...])
        act[0:16, :] = norm_rows(temporal, dgain_ref[...]).astype(BF)

        wide = dot(act[0:16, :], exp_v[:, 0:256])
        for at in range(0, FF, 256):
            hidden = gelu(wide).astype(BF)
            if at + 256 < FF:
                wide = dot(act[0:16, :], exp_v[:, at + 256:at + 512])
            temporal = temporal + dot(hidden, red_v[at:at + 256, :])

        for section in range(4):
            obuf[section] = temporal[8:16, 256 * section:256 * section + 256]
        for section in range(3):
            result_copy(section).start()
        out_ref[...] = obuf[3, MINE - 8:MINE - 8 + NF, :]
        for section in range(3):
            result_copy(section).wait_send()

    @pl.when(seg == 2)
    def _():
        for f in range(NF):
            for d in range(-REACH, REACH + 1):
                pool_copy(f, d).wait_send()

    @pl.when(seg < 2)
    def _():
        for f in range(NF):
            relay(f).wait_send()

    @pl.when(seg == 0)
    def _():
        for f in range(NF):
            early(f).wait_send()

    @pl.when(seg == 3)
    def _():
        for f in range(NF):
            partial(f).wait_send()

    @pl.when((seg == 0) & (core == 1))
    def _():
        for kind in range(2):
            shard(kind).wait_send()

    @pl.when(active)
    def _():
        half_drain()

    @pl.when(seg > 0)
    def _():
        full_drain()

    @pl.when(seg < 3)
    def _():
        result_copy(0).wait_recv()
        out_ref[...] = rbuf[MINE - 8:MINE - 8 + NF, :]


def body(frames, triple_weight, output_weight, expand_weight, reduce_weight, attend_gain, dense_gain, final_gain, shot_lengths):
    vmem = pl.BlockSpec(memory_space=pltpu.VMEM)
    anywhere = pl.BlockSpec(memory_space=pl.ANY)
    dma = pltpu.SemaphoreType.DMA
    return pl.pallas_call(
        kernel,
        out_shape=jax.ShapeDtypeStruct((NF, 256), F32),
        in_specs=[vmem, anywhere, anywhere, anywhere, anywhere, vmem, vmem, vmem,
                  pl.BlockSpec(memory_space=pltpu.SMEM)],
        out_specs=vmem,
        scratch_shapes=[
            pltpu.VMEM((D, FF), BF), pltpu.VMEM((FF, D), BF),
            pltpu.VMEM((D, FF // 2), BF), pltpu.VMEM((FF // 2, D), BF), pltpu.VMEM((D, 3 * D), BF), pltpu.VMEM((D, D), BF),
            pltpu.VMEM((NF, PAD, D), F32), pltpu.VMEM((NF, PAD, D), BF), pltpu.VMEM((NF, PAD, D), BF),
            pltpu.VMEM((NF, PAD, D), BF), pltpu.VMEM((NF, PAD, D), BF),
            pltpu.VMEM((PAD, 3 * D), BF), pltpu.VMEM((PAD, D), BF), pltpu.VMEM((PAD, D), BF),
            pltpu.VMEM((NF, 8, 128), F32), pltpu.VMEM((SLOTS, NF, 8, 128), F32), pltpu.VMEM((4, 8, 256), F32), pltpu.VMEM((8, 256), F32),
            dma((4,)), dma((2, 4, 4, 2)), dma((2, 4, 4, 2)), dma((2, 4, 4)), dma((2, 4, 4)),
            dma((2, 4, 4, 2)), dma((2, 4, 4, 2)), dma((2, 4, 4)), dma((2, 4, 4)),
            dma((NF,)), dma((NF,)), dma((NF,)), dma((NF,)), dma((NF,)), dma((2,)), dma((2,)),
            dma((NF, SLOTS)), dma((NF, SLOTS)), dma((3,)), dma(()),
        ],
        compiler_params=pltpu.CompilerParams(
            collective_id=0, has_side_effects=True, vmem_limit_bytes=60 * 1024 * 1024),
    )(frames, triple_weight, output_weight, expand_weight, reduce_weight, attend_gain, dense_gain,
      final_gain.reshape(1, D), shot_lengths)


def solution(mesh):
    return jax.shard_map(
        body,
        mesh=mesh,
        in_specs=(
            P("lane", None, None),
            P("segment", None, None),
            P("segment", None, None),
            P("segment", None, "lane"),
            P("segment", "lane", None),
            P("segment", None),
            P("segment", None),
            P(),
            P(),
        ),
        out_specs=P("lane", "segment"),
        check_vma=False,
    )
```

```python
import functools
import math

import jax
import jax.numpy as jnp
from jax import lax
from jax.experimental import pallas as pl
from jax.experimental.pallas import tpu as pltpu
from jax.sharding import PartitionSpec as P

HEADS = 16
ROWS = 197
PAD = 208
SENT = 200
D = 1024
FF = 4096
NF = 3
REACH = 4
SLOTS = 2 * REACH + 1
KEYS = 32
MINE = NF * REACH
MESH = pl.DeviceIdType.MESH
F32 = jnp.float32
BF = jnp.bfloat16


def dot(a, b):
    return lax.dot_general(a, b, (((1,), (0,)), ((), ())), preferred_element_type=F32)


def dot_t(a, b):
    return lax.dot_general(a, b, (((1,), (1,)), ((), ())), preferred_element_type=F32)


def gelu(x):
    return 0.5 * x * (1.0 + lax.erf(x * (1.0 / math.sqrt(2.0))))


def norm_rows(x, gain):
    average = jnp.mean(x, axis=-1, keepdims=True)
    centred = x - average
    spread = jnp.mean(centred * centred, axis=-1, keepdims=True)
    return centred * lax.rsqrt(spread + 1e-06) * gain


def kernel(
    frames_hbm, triple_hbm, output_hbm, expand_hbm, reduce_hbm, again_ref, dgain_ref, fgain_ref, shot_ref,
    out_ref,
    exp_v, red_v, exp_h, red_h, trip_v, outw_v, frames_v, hid, state, inb, outb, outy, packed, act, ctx, pooled, pin, obuf, rbuf,
    local_sem, send_sem, recv_sem, sib_send, sib_recv, hsend_sem, hrecv_sem, hsib_send, hsib_recv,
    rel_send, rel_recv, early_send, early_recv, shard_send, shard_recv,
    pool_send, pool_recv, fin_send, fin_recv,
):
    seg = lax.axis_index("segment")
    lane = lax.axis_index("lane")
    cx = lane // 8
    cz = (lane // 2) % 4
    core = lane % 2

    def lane_at(x, z, c):
        return ((x % 4) * 4 + (z % 4)) * 2 + c

    loads = [
        pltpu.make_async_copy(triple_hbm.at[0], trip_v, local_sem.at[0]),
        pltpu.make_async_copy(output_hbm.at[0], outw_v, local_sem.at[1]),
        pltpu.make_async_copy(frames_hbm, frames_v, local_sem.at[4]),
    ]
    for copy in loads:
        copy.start()

    for f in range(NF):
        for way in range(2):
            inb[way, f, 192:PAD, :] = jnp.zeros((PAD - 192, D), BF)

    peers = [
        (seg, lane_at(cx + 1, cz, core)), (seg, lane_at(cx + 3, cz, core)),
        (seg, lane_at(cx, cz + 1, core)), (seg, lane_at(cx, cz + 3, core)),
        (seg, lane_at(cx, cz, 1 - core)),
        ((seg + 1) % 4, lane), ((seg + 2) % 4, lane), ((seg + 3) % 4, lane),
    ]
    barrier = pltpu.get_barrier_semaphore()
    for peer in peers:
        pl.semaphore_signal(barrier, inc=1, device_id=peer, device_id_type=MESH)
    pl.semaphore_wait(barrier, len(peers))

    own_src = (expand_hbm.at[0], reduce_hbm.at[0])

    def pane(exp_ref, red_ref, kind, owner, half):
        if kind == 0:
            cols = pl.ds(pl.multiple_of(owner * 128, 128), 128)
            rows = pl.ds(0, D) if half is None else pl.ds(half * (D // 2), D // 2)
            return exp_ref.at[rows, cols]
        if half is None:
            return red_ref.at[pl.ds(pl.multiple_of(owner * 128, 128), 128), :]
        return red_ref.at[pl.ds(pl.multiple_of(owner * 128 + half * 64, 64), 64), :]

    def make_ring(exp_ref, red_ref, halved, ssem, rsem, bsend, brecv):
        def region(kind, dp, dq, c, half):
            x, z = (cx + dp + 4, cz + dq + 4) if kind == 0 else (cx + dq + 4, cz + dp + 4)
            owner = lane_at(x, z, 0) // 2 if halved else lane_at(x, z, c)
            return pane(exp_ref, red_ref, kind, owner, half)

        def neighbour(kind, along_p, sign):
            s = sign + 4
            if (kind == 0) == along_p:
                return (seg, lane_at(cx + s, cz, core))
            return (seg, lane_at(cx, cz + s, core))

        def source(kind, dp, dq, dst):
            return own_src[kind] if dp == 0 and dq == 0 and not halved else dst

        def hop(kind, dp, dq, half, along_p, sign):
            rp, rq = (dp - sign, dq) if along_p else (dp, dq - sign)
            h = half or 0
            dst = region(kind, dp, dq, core, half)
            return pltpu.make_async_remote_copy(
                src_ref=source(kind, dp, dq, dst), dst_ref=dst,
                send_sem=ssem.at[kind, rp % 4, rq % 4, h], recv_sem=rsem.at[kind, rp % 4, rq % 4, h],
                device_id=neighbour(kind, along_p, sign), device_id_type=MESH)

        def arrival(kind, rp, rq, half):
            h = half or 0
            dst = region(kind, rp, rq, core, half)
            return pltpu.make_async_remote_copy(
                src_ref=dst, dst_ref=dst,
                send_sem=ssem.at[kind, rp % 4, rq % 4, h], recv_sem=rsem.at[kind, rp % 4, rq % 4, h],
                device_id=neighbour(kind, True, 1), device_id_type=MESH)

        def sibling(kind, dp, dq, receive=False):
            dst = region(kind, dp, dq, 1 - core if receive else core, None)
            return pltpu.make_async_remote_copy(
                src_ref=dst if receive else source(kind, dp, dq, dst), dst_ref=dst,
                send_sem=bsend.at[kind, dp % 4, dq % 4], recv_sem=brecv.at[kind, dp % 4, dq % 4],
                device_id=(seg, lane_at(cx, cz, 1 - core)), device_id_type=MESH)

        sent = []

        def go(make, *args):
            make(*args).start()
            if (make, args) not in sent:
                sent.append((make, args))

        def start(ready=None):
            for kind in range(2):
                if ready is not None:
                    ready(kind)
                for sign in (1, -1):
                    go(hop, kind, 0, 0, None, True, sign)
            for kind in range(2):
                for sign in (1, -1):
                    go(hop, kind, 0, 0, None, False, sign)
                go(sibling, kind, 0, 0)

        def spread(kind, dp):
            for sign in (1, -1):
                go(hop, kind, dp, 0, None, False, sign)
            go(sibling, kind, dp, 0)

        def ev_p(kind, rp):
            arrival(kind, rp, 0, None).wait_recv()
            go(hop, kind, rp, 0, 0 if rp < 0 else 1, True, -rp)
            spread(kind, rp)

        def ev_p2(kind):
            arrival(kind, 2, 0, 0).wait_recv()
            arrival(kind, 2, 0, 1).wait_recv()
            spread(kind, 2)

        def ev_q(kind, rp, rq):
            arrival(kind, rp, rq, None).wait_recv()
            go(hop, kind, rp, rq, 0 if rq < 0 else 1, False, -rq)
            go(sibling, kind, rp, rq)

        def ev_q2(kind, rp):
            arrival(kind, rp, 2, 0).wait_recv()
            arrival(kind, rp, 2, 1).wait_recv()
            go(sibling, kind, rp, 2)

        events = []

        def both(fn, *args):
            for kind in range(2):
                events.append(functools.partial(fn, kind, *args))

        both(ev_p, -1)
        both(ev_p, 1)
        both(ev_q, 0, -1)
        both(ev_q, 0, 1)
        both(ev_p2)
        both(ev_q, -1, -1)
        both(ev_q, -1, 1)
        both(ev_q, 1, -1)
        both(ev_q, 1, 1)
        both(ev_q2, 0)
        both(ev_q, 2, -1)
        both(ev_q, 2, 1)
        both(ev_q2, -1)
        both(ev_q2, 1)
        both(ev_q2, 2)

        def pump(count):
            for _ in range(min(count, len(events))):
                events.pop(0)()

        def from_sibling():
            for kind in range(2):
                for dp in range(4):
                    for dq in range(4):
                        sibling(kind, dp, dq, True).wait_recv()

        def drain():
            for make, args in sent:
                make(*args).wait_send()

        return start, pump, from_sibling, drain

    full_start, full_pump, full_sibling, full_drain = make_ring(
        exp_v, red_v, False, send_sem, recv_sem, sib_send, sib_recv)
    half_start, half_pump, half_sibling, half_drain = make_ring(
        exp_h, red_h, True, hsend_sem, hrecv_sem, hsib_send, hsib_recv)

    halves = (seg == 0) | (seg == 3)
    active = ((seg == 0) & (core == 0)) | ((seg == 3) & (core == 1))

    def shard(kind):
        return pltpu.make_async_remote_copy(
            src_ref=own_src[kind], dst_ref=pane(exp_h, red_h, kind, lane // 2, None),
            send_sem=shard_send.at[kind], recv_sem=shard_recv.at[kind],
            device_id=((seg + 3) % 4, lane), device_id_type=MESH)

    def own_load(kind, exp_ref, red_ref, owner):
        return pltpu.make_async_copy(own_src[kind], pane(exp_ref, red_ref, kind, owner, None), local_sem.at[2 + kind])

    @pl.when((seg == 0) & (core == 1))
    def _():
        for kind in range(2):
            shard(kind).start()

    @pl.when((seg == 0) & (core == 0))
    def _():
        for kind in range(2):
            own_load(kind, exp_h, red_h, lane // 2).start()

    def ready(kind):
        @pl.when(seg == 0)
        def _():
            own_load(kind, exp_h, red_h, lane // 2).wait()

        @pl.when(seg == 3)
        def _():
            shard(kind).wait_recv()

    @pl.when(active)
    def _():
        half_start(ready)

    def norm_into(f, gain_ref):
        gain = gain_ref[...]
        for i in range(PAD // 16):
            rows = pl.ds(16 * i, 16)
            act[rows, :] = norm_rows(state[f, rows, :], gain).astype(BF)

    def project(f):
        norm_into(f, again_ref)

        for at in range(0, 3 * D, 256):
            packed[:, at:at + 256] = dot(act[...], trip_v[:, at:at + 256]).astype(BF)

    def attend():
        low = lax.broadcasted_iota(jnp.int32, (PAD, 128), 1) < 64
        bias = jnp.where(lax.broadcasted_iota(jnp.int32, (1, PAD), 1) < ROWS, 0.0, -1e30).astype(F32)

        for at in range(0, D, 128):
            q = packed[:, at:at + 128]
            k = packed[:, D + at:D + at + 128]
            v = packed[:, 2 * D + at:2 * D + at + 128]
            parts = []
            for keep in (low, ~low):
                scores = dot_t(jnp.where(keep, q * 0.125, 0.0).astype(BF), k) + bias
                shares = jnp.exp(scores - jnp.max(scores, axis=-1, keepdims=True))
                total = jnp.sum(shares, axis=-1, keepdims=True)
                parts.append(dot(shares.astype(BF), v) / total)
            ctx[:, at:at + 128] = jnp.where(low, parts[0], parts[1]).astype(BF)

    def join(f):
        for at in range(0, D, 256):
            state[f, :, at:at + 256] += dot(ctx[...], outw_v[:, at:at + 256])

    def feed(f, exp_ref, red_ref, depth, emit):
        wide = dot(act[...], exp_ref[:, 0:256])
        for at in range(0, depth, 256):
            hidden = gelu(wide).astype(BF)
            if at + 256 < depth:
                wide = dot(act[...], exp_ref[:, at + 256:at + 512])
            hid[:, at:at + 256] = hidden
        for c in range(4):
            cols = slice(256 * c, 256 * c + 256)
            emit(c, cols, state[f, :, cols] + dot(hid[:, 0:depth], red_ref[:, cols]))

    for copy in loads:
        copy.wait()

    def relay(f, c, way, section):
        cols = slice(256 * c, 256 * c + 256)
        return pltpu.make_async_remote_copy(
            src_ref=outb.at[f, 0:SENT, cols], dst_ref=inb.at[way, f, 0:SENT, cols],
            send_sem=rel_send.at[f, c], recv_sem=rel_recv.at[way, f, c],
            device_id=(section, lane), device_id_type=MESH)

    def pass_on(f, way, section):
        def emit(c, cols, value):
            outb[f, :, cols] = value.astype(BF)
            relay(f, c, way, section).start()

        return emit

    def early(f):
        return pltpu.make_async_remote_copy(
            src_ref=outy.at[f, 0:SENT, :], dst_ref=inb.at[0, f, 0:SENT, :], send_sem=early_send.at[f], recv_sem=early_recv.at[f],
            device_id=((seg + 3) % 4, lane), device_id_type=MESH)

    @pl.when(halves)
    def _():
        for f in range(NF):
            @pl.when(seg == 0)
            def _():
                state[f, 192:PAD, :] = jnp.zeros((PAD - 192, D), F32)
                state[f, 0:ROWS, :] = frames_v[f].astype(F32)
                project(f)

            @pl.when(active)
            def _():
                half_pump(4)

            @pl.when(seg == 0)
            def _():
                attend()

            @pl.when(active)
            def _():
                half_pump(4)

            @pl.when(seg == 0)
            def _():
                join(f)
                norm_into(f, dgain_ref)
                outy[f] = act[...]
                early(f).start()

            @pl.when(active)
            def _():
                half_pump(2)

        @pl.when(active)
        def _():
            half_pump(1000)

        @pl.when(~active)
        def _():
            half_sibling()

        @pl.when(seg == 3)
        def _():
            full_start()

        def step(f, carry):
            @pl.when(seg == 3)
            def _():
                early(f).wait_recv()
                act[...] = inb[0, f]
                state[f] = jnp.zeros((PAD, D), F32)

            @pl.when(seg == 0)
            def _():
                act[...] = outy[f]

            feed(f, exp_h, red_h, FF // 2, pass_on(f, seg // 3, 1))
            return carry

        lax.fori_loop(0, NF, step, 0)

    @pl.when((seg == 1) | (seg == 2))
    def _():
        full_start()

    @pl.when(seg > 0)
    def _():
        for kind in range(2):
            own_load(kind, exp_v, red_v, lane).start()
        full_pump(1000)

    def gathered():
        full_sibling()
        for kind in range(2):
            own_load(kind, exp_v, red_v, lane).wait()

    def pool_copy(f, d):
        return pltpu.make_async_remote_copy(
            src_ref=pooled.at[f], dst_ref=pin.at[d + REACH, f],
            send_sem=pool_send.at[f, d + REACH], recv_sem=pool_recv.at[f, d + REACH],
            device_id=((seg + 1) % 4, (lane - d + 32) % 32), device_id_type=MESH)

    @pl.when((seg == 1) | (seg == 2))
    def _():
        def step(f, carry):
            for c in range(4):
                relay(f, c, 0, 2).wait_recv()

            @pl.when(seg == 2)
            def _():
                state[f] = inb[0, f].astype(F32)

            @pl.when(seg == 1)
            def _():
                for c in range(4):
                    relay(f, c, 1, 2).wait_recv()
                state[f] = inb[0, f].astype(F32) + inb[1, f].astype(F32)

            project(f)
            attend()
            join(f)
            norm_into(f, dgain_ref)

            @pl.when(f == 0)
            def _():
                gathered()

            @pl.when(seg == 1)
            def _():
                feed(f, exp_v, red_v, FF, pass_on(f, 0, 2))

            @pl.when(seg == 2)
            def _():
                def keep_block(c, cols, value):
                    state[f, :, cols] = value

                feed(f, exp_v, red_v, FF, keep_block)
                gain = fgain_ref[...]
                total = jnp.zeros((16, D), F32)
                for i in range(PAD // 16):
                    rows = norm_rows(state[f, pl.ds(16 * i, 16), :], gain)
                    if 16 * i + 16 > ROWS:
                        keep = lax.broadcasted_iota(jnp.int32, (16, D), 0) < ROWS - 16 * i
                        rows = jnp.where(keep, rows, 0.0)
                    total = total + rows
                total = jnp.sum(total, axis=0, keepdims=True) * (1.0 / ROWS)
                for j in range(8):
                    pooled[f, j:j + 1, :] = total[:, 128 * j:128 * j + 128]
                for d in range(-REACH, REACH + 1):
                    pool_copy(f, d).start()

            return carry

        lax.fori_loop(0, NF, step, 0)

    def result_copy(section):
        return pltpu.make_async_remote_copy(
            src_ref=obuf.at[section], dst_ref=rbuf, send_sem=fin_send.at[section], recv_sem=fin_recv,
            device_id=(section, lane), device_id_type=MESH)

    @pl.when(seg == 3)
    def _():
        state[0, 24:KEYS, :] = jnp.zeros((KEYS - 24, D), F32)
        for f in range(NF):
            for d in range(-REACH, REACH + 1):
                pool_copy(f, d).wait_recv()
                row = NF * (d + REACH) + f
                for j in range(8):
                    state[0, row:row + 1, 128 * j:128 * j + 128] = pin[d + REACH, f, j:j + 1, :]
        again = again_ref[...]
        for i in range(KEYS // 16):
            rows = pl.ds(16 * i, 16)
            act[rows, :] = norm_rows(state[0, rows, :], again).astype(BF)

        for at in range(0, 3 * D, 256):
            packed[0:KEYS, at:at + 256] = dot(act[0:KEYS, :], trip_v[:, at:at + 256]).astype(BF)

        col = lax.broadcasted_iota(jnp.int32, (16, KEYS), 1)
        row = lax.broadcasted_iota(jnp.int32, (16, KEYS), 0)
        key_at = (lane - REACH) * NF + col
        key_at = jnp.where(key_at < 0, key_at + 32 * NF, key_at)
        key_at = jnp.where(key_at >= 32 * NF, key_at - 32 * NF, key_at)
        own_at = lane * NF + jnp.clip(row - MINE, 0, NF - 1)
        key_shot = jnp.zeros((16, KEYS), jnp.int32)
        own_shot = jnp.zeros((16, KEYS), jnp.int32)
        end = 0
        for s in range(24):
            end = end + shot_ref[s]
            key_shot += (key_at >= end).astype(jnp.int32)
            own_shot += (own_at >= end).astype(jnp.int32)
        allowed = (key_shot == own_shot) & (col < NF * SLOTS)
        low = lax.broadcasted_iota(jnp.int32, (16, 128), 1) < 64

        for at in range(0, D, 128):
            q = packed[0:16, at:at + 128]
            k = packed[0:KEYS, D + at:D + at + 128]
            v = packed[0:KEYS, 2 * D + at:2 * D + at + 128]
            parts = []
            for keep in (low, ~low):
                scores = dot_t(jnp.where(keep, q * 0.125, 0.0).astype(BF), k)
                scores = jnp.where(allowed, scores, -1e30)
                shares = jnp.exp(scores - jnp.max(scores, axis=-1, keepdims=True))
                total = jnp.sum(shares, axis=-1, keepdims=True)
                high = shares.astype(BF)
                rest = (shares - high.astype(F32)).astype(BF)
                parts.append((dot(high, v) + dot(rest, v)) / total)
            ctx[0:16, at:at + 128] = jnp.where(low, parts[0], parts[1]).astype(BF)

        temporal = state[0, 0:16, :] + dot(ctx[0:16, :], outw_v[...])
        act[0:16, :] = norm_rows(temporal, dgain_ref[...]).astype(BF)

        gathered()
        wide = dot(act[0:16, :], exp_v[:, 0:256])
        for at in range(0, FF, 256):
            hidden = gelu(wide).astype(BF)
            if at + 256 < FF:
                wide = dot(act[0:16, :], exp_v[:, at + 256:at + 512])
            temporal = temporal + dot(hidden, red_v[at:at + 256, :])

        for section in range(4):
            obuf[section] = temporal[8:16, 256 * section:256 * section + 256]
        for section in range(3):
            result_copy(section).start()
        out_ref[...] = obuf[3, MINE - 8:MINE - 8 + NF, :]
        for section in range(3):
            result_copy(section).wait_send()

    @pl.when(seg == 2)
    def _():
        for f in range(NF):
            for d in range(-REACH, REACH + 1):
                pool_copy(f, d).wait_send()

    @pl.when(seg < 2)
    def _():
        for f in range(NF):
            for c in range(4):
                relay(f, c, 0, 1).wait_send()

    @pl.when(seg == 0)
    def _():
        for f in range(NF):
            early(f).wait_send()

    @pl.when(seg == 3)
    def _():
        for f in range(NF):
            for c in range(4):
                relay(f, c, 1, 1).wait_send()

    @pl.when((seg == 0) & (core == 1))
    def _():
        for kind in range(2):
            shard(kind).wait_send()

    @pl.when(active)
    def _():
        half_drain()

    @pl.when(seg > 0)
    def _():
        full_drain()

    @pl.when(seg < 3)
    def _():
        result_copy(0).wait_recv()
        out_ref[...] = rbuf[MINE - 8:MINE - 8 + NF, :]


def body(frames, triple_weight, output_weight, expand_weight, reduce_weight, attend_gain, dense_gain, final_gain, shot_lengths):
    vmem = pl.BlockSpec(memory_space=pltpu.VMEM)
    anywhere = pl.BlockSpec(memory_space=pl.ANY)
    dma = pltpu.SemaphoreType.DMA
    return pl.pallas_call(
        kernel,
        out_shape=jax.ShapeDtypeStruct((NF, 256), F32),
        in_specs=[anywhere, anywhere, anywhere, anywhere, anywhere, vmem, vmem, vmem,
                  pl.BlockSpec(memory_space=pltpu.SMEM)],
        out_specs=vmem,
        scratch_shapes=[
            pltpu.VMEM((D, FF), BF), pltpu.VMEM((FF, D), BF),
            pltpu.VMEM((D, FF // 2), BF), pltpu.VMEM((FF // 2, D), BF), pltpu.VMEM((D, 3 * D), BF), pltpu.VMEM((D, D), BF),
            pltpu.VMEM((NF, ROWS, D), BF), pltpu.VMEM((PAD, FF), BF),
            pltpu.VMEM((NF, PAD, D), F32), pltpu.VMEM((2, NF, PAD, D), BF),
            pltpu.VMEM((NF, PAD, D), BF), pltpu.VMEM((NF, PAD, D), BF),
            pltpu.VMEM((PAD, 3 * D), BF), pltpu.VMEM((PAD, D), BF), pltpu.VMEM((PAD, D), BF),
            pltpu.VMEM((NF, 8, 128), F32), pltpu.VMEM((SLOTS, NF, 8, 128), F32), pltpu.VMEM((4, 8, 256), F32), pltpu.VMEM((8, 256), F32),
            dma((5,)), dma((2, 4, 4, 2)), dma((2, 4, 4, 2)), dma((2, 4, 4)), dma((2, 4, 4)),
            dma((2, 4, 4, 2)), dma((2, 4, 4, 2)), dma((2, 4, 4)), dma((2, 4, 4)),
            dma((NF, 4)), dma((2, NF, 4)), dma((NF,)), dma((NF,)), dma((2,)), dma((2,)),
            dma((NF, SLOTS)), dma((NF, SLOTS)), dma((3,)), dma(()),
        ],
        compiler_params=pltpu.CompilerParams(
            collective_id=0, has_side_effects=True, vmem_limit_bytes=60 * 1024 * 1024),
    )(frames, triple_weight, output_weight, expand_weight, reduce_weight, attend_gain, dense_gain,
      final_gain.reshape(1, D), shot_lengths)


def solution(mesh):
    return jax.shard_map(
        body,
        mesh=mesh,
        in_specs=(
            P("lane", None, None),
            P("segment", None, None),
            P("segment", None, None),
            P("segment", None, "lane"),
            P("segment", "lane", None),
            P("segment", None),
            P("segment", None),
            P(),
            P(),
        ),
        out_specs=P("lane", "segment"),
        check_vma=False,
    )
```

```python
import functools
import math

import jax
import jax.numpy as jnp
from jax import lax
from jax.experimental import pallas as pl
from jax.experimental.pallas import tpu as pltpu
from jax.sharding import PartitionSpec as P

HEADS = 16
ROWS = 197
PAD = 208
SENT = 200
BLOCKS = 2
WIDE = 1024 // BLOCKS
D = 1024
FF = 4096
NF = 3
REACH = 4
SLOTS = 2 * REACH + 1
KEYS = 32
MINE = NF * REACH
MESH = pl.DeviceIdType.MESH
F32 = jnp.float32
BF = jnp.bfloat16


def dot(a, b):
    return lax.dot_general(a, b, (((1,), (0,)), ((), ())), preferred_element_type=F32)


def dot_t(a, b):
    return lax.dot_general(a, b, (((1,), (1,)), ((), ())), preferred_element_type=F32)


def gelu(x):
    return 0.5 * x * (1.0 + lax.erf(x * (1.0 / math.sqrt(2.0))))


def norm_rows(x, gain):
    average = jnp.mean(x, axis=-1, keepdims=True)
    centred = x - average
    spread = jnp.mean(centred * centred, axis=-1, keepdims=True)
    return centred * lax.rsqrt(spread + 1e-06) * gain


def kernel(
    frames_hbm, triple_hbm, output_hbm, expand_hbm, reduce_hbm, again_ref, dgain_ref, fgain_ref, shot_ref,
    out_ref,
    exp_v, red_v, exp_h, red_h, trip_v, outw_v, frames_v, hid, state, inb, outb, outy, packed, act, ctx, pooled, pin, obuf, rbuf,
    local_sem, send_sem, recv_sem, sib_send, sib_recv, hsend_sem, hrecv_sem, hsib_send, hsib_recv,
    rel_send, rel_recv, early_send, early_recv, shard_send, shard_recv,
    pool_send, pool_recv, fin_send, fin_recv,
):
    seg = lax.axis_index("segment")
    lane = lax.axis_index("lane")
    cx = lane // 8
    cz = (lane // 2) % 4
    core = lane % 2

    def lane_at(x, z, c):
        return ((x % 4) * 4 + (z % 4)) * 2 + c

    loads = [
        pltpu.make_async_copy(triple_hbm.at[0], trip_v, local_sem.at[0]),
        pltpu.make_async_copy(output_hbm.at[0], outw_v, local_sem.at[1]),
        pltpu.make_async_copy(frames_hbm, frames_v, local_sem.at[4]),
    ]
    for copy in loads:
        copy.start()

    for f in range(NF):
        for way in range(2):
            inb[way, f, 192:PAD, :] = jnp.zeros((PAD - 192, D), BF)

    peers = [
        (seg, lane_at(cx + 1, cz, core)), (seg, lane_at(cx + 3, cz, core)),
        (seg, lane_at(cx, cz + 1, core)), (seg, lane_at(cx, cz + 3, core)),
        (seg, lane_at(cx, cz, 1 - core)),
        ((seg + 1) % 4, lane), ((seg + 3) % 4, lane),
    ]
    barrier = pltpu.get_barrier_semaphore()
    for peer in peers:
        pl.semaphore_signal(barrier, inc=1, device_id=peer, device_id_type=MESH)
    pl.semaphore_wait(barrier, len(peers))

    own_src = (expand_hbm.at[0], reduce_hbm.at[0])

    def pane(exp_ref, red_ref, kind, owner, half):
        if kind == 0:
            cols = pl.ds(pl.multiple_of(owner * 128, 128), 128)
            rows = pl.ds(0, D) if half is None else pl.ds(half * (D // 2), D // 2)
            return exp_ref.at[rows, cols]
        if half is None:
            return red_ref.at[pl.ds(pl.multiple_of(owner * 128, 128), 128), :]
        return red_ref.at[pl.ds(pl.multiple_of(owner * 128 + half * 64, 64), 64), :]

    def make_ring(exp_ref, red_ref, halved, ssem, rsem, bsend, brecv):
        def region(kind, dp, dq, c, half):
            x, z = (cx + dp + 4, cz + dq + 4) if kind == 0 else (cx + dq + 4, cz + dp + 4)
            owner = lane_at(x, z, 0) // 2 if halved else lane_at(x, z, c)
            return pane(exp_ref, red_ref, kind, owner, half)

        def neighbour(kind, along_p, sign):
            s = sign + 4
            if (kind == 0) == along_p:
                return (seg, lane_at(cx + s, cz, core))
            return (seg, lane_at(cx, cz + s, core))

        def source(kind, dp, dq, dst):
            return own_src[kind] if dp == 0 and dq == 0 and not halved else dst

        def hop(kind, dp, dq, half, along_p, sign):
            rp, rq = (dp - sign, dq) if along_p else (dp, dq - sign)
            h = half or 0
            dst = region(kind, dp, dq, core, half)
            return pltpu.make_async_remote_copy(
                src_ref=source(kind, dp, dq, dst), dst_ref=dst,
                send_sem=ssem.at[kind, rp % 4, rq % 4, h], recv_sem=rsem.at[kind, rp % 4, rq % 4, h],
                device_id=neighbour(kind, along_p, sign), device_id_type=MESH)

        def arrival(kind, rp, rq, half):
            h = half or 0
            dst = region(kind, rp, rq, core, half)
            return pltpu.make_async_remote_copy(
                src_ref=dst, dst_ref=dst,
                send_sem=ssem.at[kind, rp % 4, rq % 4, h], recv_sem=rsem.at[kind, rp % 4, rq % 4, h],
                device_id=neighbour(kind, True, 1), device_id_type=MESH)

        def sibling(kind, dp, dq, receive=False):
            dst = region(kind, dp, dq, 1 - core if receive else core, None)
            return pltpu.make_async_remote_copy(
                src_ref=dst if receive else source(kind, dp, dq, dst), dst_ref=dst,
                send_sem=bsend.at[kind, dp % 4, dq % 4], recv_sem=brecv.at[kind, dp % 4, dq % 4],
                device_id=(seg, lane_at(cx, cz, 1 - core)), device_id_type=MESH)

        sent = []

        def go(make, *args):
            make(*args).start()
            if (make, args) not in sent:
                sent.append((make, args))

        def start(ready=None):
            for kind in range(2):
                if ready is not None:
                    ready(kind)
                for sign in (1, -1):
                    go(hop, kind, 0, 0, None, True, sign)
                if ready is not None:
                    for sign in (1, -1):
                        go(hop, kind, 0, 0, None, False, sign)
            for kind in range(2):
                if ready is None:
                    for sign in (1, -1):
                        go(hop, kind, 0, 0, None, False, sign)
                go(sibling, kind, 0, 0)

        def spread(kind, dp):
            for sign in (1, -1):
                go(hop, kind, dp, 0, None, False, sign)
            go(sibling, kind, dp, 0)

        def ev_p(kind, rp):
            arrival(kind, rp, 0, None).wait_recv()
            go(hop, kind, rp, 0, 0 if rp < 0 else 1, True, -rp)
            spread(kind, rp)

        def ev_p2(kind):
            arrival(kind, 2, 0, 0).wait_recv()
            arrival(kind, 2, 0, 1).wait_recv()
            spread(kind, 2)

        def ev_q(kind, rp, rq):
            arrival(kind, rp, rq, None).wait_recv()
            go(hop, kind, rp, rq, 0 if rq < 0 else 1, False, -rq)
            go(sibling, kind, rp, rq)

        def ev_q2(kind, rp):
            arrival(kind, rp, 2, 0).wait_recv()
            arrival(kind, rp, 2, 1).wait_recv()
            go(sibling, kind, rp, 2)

        events = []

        def both(fn, *args):
            for kind in range(2):
                events.append(functools.partial(fn, kind, *args))

        both(ev_p, -1)
        both(ev_p, 1)
        both(ev_q, 0, -1)
        both(ev_q, 0, 1)
        both(ev_p2)
        both(ev_q, -1, -1)
        both(ev_q, -1, 1)
        both(ev_q, 1, -1)
        both(ev_q, 1, 1)
        both(ev_q2, 0)
        both(ev_q, 2, -1)
        both(ev_q, 2, 1)
        both(ev_q2, -1)
        both(ev_q2, 1)
        both(ev_q2, 2)

        def pump(count):
            for _ in range(min(count, len(events))):
                events.pop(0)()

        def from_sibling():
            for kind in range(2):
                for dp in range(4):
                    for dq in range(4):
                        sibling(kind, dp, dq, True).wait_recv()

        def drain():
            for make, args in sent:
                make(*args).wait_send()

        return start, pump, from_sibling, drain

    full_start, full_pump, full_sibling, full_drain = make_ring(
        exp_v, red_v, False, send_sem, recv_sem, sib_send, sib_recv)
    half_start, half_pump, half_sibling, half_drain = make_ring(
        exp_h, red_h, True, hsend_sem, hrecv_sem, hsib_send, hsib_recv)

    halves = (seg == 0) | (seg == 3)
    active = ((seg == 0) & (core == 0)) | ((seg == 3) & (core == 1))

    def shard(kind):
        return pltpu.make_async_remote_copy(
            src_ref=own_src[kind], dst_ref=pane(exp_h, red_h, kind, lane // 2, None),
            send_sem=shard_send.at[kind], recv_sem=shard_recv.at[kind],
            device_id=((seg + 3) % 4, lane), device_id_type=MESH)

    def own_load(kind, exp_ref, red_ref, owner):
        return pltpu.make_async_copy(own_src[kind], pane(exp_ref, red_ref, kind, owner, None), local_sem.at[2 + kind])

    @pl.when((seg == 0) & (core == 1))
    def _():
        for kind in range(2):
            shard(kind).start()

    @pl.when((seg == 0) & (core == 0))
    def _():
        for kind in range(2):
            own_load(kind, exp_h, red_h, lane // 2).start()

    def ready(kind):
        @pl.when(seg == 0)
        def _():
            own_load(kind, exp_h, red_h, lane // 2).wait()

        @pl.when(seg == 3)
        def _():
            shard(kind).wait_recv()

    @pl.when(active)
    def _():
        half_start(ready)

    def norm_into(f, gain_ref):
        gain = gain_ref[...]
        for i in range(PAD // 16):
            rows = pl.ds(16 * i, 16)
            act[rows, :] = norm_rows(state[f, rows, :], gain).astype(BF)

    def project(f):
        norm_into(f, again_ref)

        for at in range(0, 3 * D, 256):
            packed[:, at:at + 256] = dot(act[...], trip_v[:, at:at + 256]).astype(BF)

    def attend():
        low = lax.broadcasted_iota(jnp.int32, (PAD, 128), 1) < 64
        bias = jnp.where(lax.broadcasted_iota(jnp.int32, (1, PAD), 1) < ROWS, 0.0, -1e30).astype(F32)

        for at in range(0, D, 128):
            q = packed[:, at:at + 128]
            k = packed[:, D + at:D + at + 128]
            v = packed[:, 2 * D + at:2 * D + at + 128]
            parts = []
            for keep in (low, ~low):
                scores = dot_t(jnp.where(keep, q * 0.125, 0.0).astype(BF), k) + bias
                shares = jnp.exp(scores - jnp.max(scores, axis=-1, keepdims=True))
                total = jnp.sum(shares, axis=-1, keepdims=True)
                parts.append(dot(shares.astype(BF), v) / total)
            ctx[:, at:at + 128] = jnp.where(low, parts[0], parts[1]).astype(BF)

    def join(f):
        for at in range(0, D, 256):
            state[f, :, at:at + 256] += dot(ctx[...], outw_v[:, at:at + 256])

    def feed(f, exp_ref, red_ref, depth, emit):
        wide = dot(act[...], exp_ref[:, 0:256])
        for at in range(0, depth, 256):
            hidden = gelu(wide).astype(BF)
            if at + 256 < depth:
                wide = dot(act[...], exp_ref[:, at + 256:at + 512])
            hid[:, at:at + 256] = hidden
        for c in range(BLOCKS):
            cols = slice(WIDE * c, WIDE * c + WIDE)
            emit(c, cols, state[f, :, cols] + dot(hid[:, 0:depth], red_ref[:, cols]))

    for copy in loads:
        copy.wait()

    def relay(f, c, way, section):
        cols = slice(WIDE * c, WIDE * c + WIDE)
        return pltpu.make_async_remote_copy(
            src_ref=outb.at[f, 0:SENT, cols], dst_ref=inb.at[way, f, 0:SENT, cols],
            send_sem=rel_send.at[f, c], recv_sem=rel_recv.at[way, f, c],
            device_id=(section, lane), device_id_type=MESH)

    def pass_on(f, way, section):
        def emit(c, cols, value):
            outb[f, :, cols] = value.astype(BF)
            relay(f, c, way, section).start()

        return emit

    def early(f):
        return pltpu.make_async_remote_copy(
            src_ref=outy.at[f, 0:SENT, :], dst_ref=inb.at[0, f, 0:SENT, :], send_sem=early_send.at[f], recv_sem=early_recv.at[f],
            device_id=((seg + 3) % 4, lane), device_id_type=MESH)

    @pl.when(halves)
    def _():
        for f in range(NF):
            @pl.when(seg == 0)
            def _():
                state[f, 192:PAD, :] = jnp.zeros((PAD - 192, D), F32)
                state[f, 0:ROWS, :] = frames_v[f].astype(F32)
                project(f)

            @pl.when(active)
            def _():
                half_pump(4)

            @pl.when(seg == 0)
            def _():
                attend()

            @pl.when(active)
            def _():
                half_pump(4)

            @pl.when(seg == 0)
            def _():
                join(f)
                norm_into(f, dgain_ref)
                outy[f] = act[...]
                early(f).start()

            @pl.when(active)
            def _():
                half_pump(2)

        @pl.when(active)
        def _():
            half_pump(1000)

        @pl.when(~active)
        def _():
            half_sibling()

        @pl.when(seg == 3)
        def _():
            full_start()

        def step(f, carry):
            @pl.when(seg == 3)
            def _():
                early(f).wait_recv()
                act[...] = inb[0, f]
                state[f] = jnp.zeros((PAD, D), F32)

            @pl.when(seg == 0)
            def _():
                act[...] = outy[f]

            feed(f, exp_h, red_h, FF // 2, pass_on(f, seg // 3, 1))
            return carry

        lax.fori_loop(0, NF, step, 0)

    @pl.when((seg == 1) | (seg == 2))
    def _():
        full_start()

    @pl.when(seg > 0)
    def _():
        for kind in range(2):
            own_load(kind, exp_v, red_v, lane).start()
        full_pump(1000)

    def gathered():
        full_sibling()
        for kind in range(2):
            own_load(kind, exp_v, red_v, lane).wait()

    def pool_copy(f, d):
        return pltpu.make_async_remote_copy(
            src_ref=pooled.at[f], dst_ref=pin.at[d + REACH, f],
            send_sem=pool_send.at[f, d + REACH], recv_sem=pool_recv.at[f, d + REACH],
            device_id=((seg + 1) % 4, (lane - d + 32) % 32), device_id_type=MESH)

    @pl.when((seg == 1) | (seg == 2))
    def _():
        def step(f, carry):
            for c in range(BLOCKS):
                relay(f, c, 0, 2).wait_recv()

            @pl.when(seg == 2)
            def _():
                state[f] = inb[0, f].astype(F32)

            @pl.when(seg == 1)
            def _():
                for c in range(BLOCKS):
                    relay(f, c, 1, 2).wait_recv()
                state[f] = inb[0, f].astype(F32) + inb[1, f].astype(F32)

            project(f)
            attend()
            join(f)
            norm_into(f, dgain_ref)

            @pl.when(f == 0)
            def _():
                gathered()

            @pl.when(seg == 1)
            def _():
                feed(f, exp_v, red_v, FF, pass_on(f, 0, 2))

            @pl.when(seg == 2)
            def _():
                def keep_block(c, cols, value):
                    state[f, :, cols] = value

                feed(f, exp_v, red_v, FF, keep_block)
                gain = fgain_ref[...]
                total = jnp.zeros((16, D), F32)
                for i in range(PAD // 16):
                    rows = norm_rows(state[f, pl.ds(16 * i, 16), :], gain)
                    if 16 * i + 16 > ROWS:
                        keep = lax.broadcasted_iota(jnp.int32, (16, D), 0) < ROWS - 16 * i
                        rows = jnp.where(keep, rows, 0.0)
                    total = total + rows
                total = jnp.sum(total, axis=0, keepdims=True) * (1.0 / ROWS)
                for j in range(8):
                    pooled[f, j:j + 1, :] = total[:, 128 * j:128 * j + 128]
                for d in range(-REACH, REACH + 1):
                    pool_copy(f, d).start()

            return carry

        lax.fori_loop(0, NF, step, 0)

    def result_copy(section):
        return pltpu.make_async_remote_copy(
            src_ref=obuf.at[section], dst_ref=rbuf, send_sem=fin_send.at[section], recv_sem=fin_recv,
            device_id=(section, lane), device_id_type=MESH)

    @pl.when(seg == 3)
    def _():
        state[0, 24:KEYS, :] = jnp.zeros((KEYS - 24, D), F32)
        for f in range(NF):
            for d in range(-REACH, REACH + 1):
                pool_copy(f, d).wait_recv()
                row = NF * (d + REACH) + f
                for j in range(8):
                    state[0, row:row + 1, 128 * j:128 * j + 128] = pin[d + REACH, f, j:j + 1, :]
        again = again_ref[...]
        for i in range(KEYS // 16):
            rows = pl.ds(16 * i, 16)
            act[rows, :] = norm_rows(state[0, rows, :], again).astype(BF)

        for at in range(0, 3 * D, 256):
            packed[0:KEYS, at:at + 256] = dot(act[0:KEYS, :], trip_v[:, at:at + 256]).astype(BF)

        col = lax.broadcasted_iota(jnp.int32, (16, KEYS), 1)
        row = lax.broadcasted_iota(jnp.int32, (16, KEYS), 0)
        key_at = (lane - REACH) * NF + col
        key_at = jnp.where(key_at < 0, key_at + 32 * NF, key_at)
        key_at = jnp.where(key_at >= 32 * NF, key_at - 32 * NF, key_at)
        own_at = lane * NF + jnp.clip(row - MINE, 0, NF - 1)
        key_shot = jnp.zeros((16, KEYS), jnp.int32)
        own_shot = jnp.zeros((16, KEYS), jnp.int32)
        end = 0
        for s in range(24):
            end = end + shot_ref[s]
            key_shot += (key_at >= end).astype(jnp.int32)
            own_shot += (own_at >= end).astype(jnp.int32)
        allowed = (key_shot == own_shot) & (col < NF * SLOTS)
        low = lax.broadcasted_iota(jnp.int32, (16, 128), 1) < 64

        for at in range(0, D, 128):
            q = packed[0:16, at:at + 128]
            k = packed[0:KEYS, D + at:D + at + 128]
            v = packed[0:KEYS, 2 * D + at:2 * D + at + 128]
            parts = []
            for keep in (low, ~low):
                scores = dot_t(jnp.where(keep, q * 0.125, 0.0).astype(BF), k)
                scores = jnp.where(allowed, scores, -1e30)
                shares = jnp.exp(scores - jnp.max(scores, axis=-1, keepdims=True))
                total = jnp.sum(shares, axis=-1, keepdims=True)
                high = shares.astype(BF)
                rest = (shares - high.astype(F32)).astype(BF)
                parts.append((dot(high, v) + dot(rest, v)) / total)
            ctx[0:16, at:at + 128] = jnp.where(low, parts[0], parts[1]).astype(BF)

        temporal = state[0, 0:16, :] + dot(ctx[0:16, :], outw_v[...])
        act[0:16, :] = norm_rows(temporal, dgain_ref[...]).astype(BF)

        gathered()
        wide = dot(act[0:16, :], exp_v[:, 0:256])
        for at in range(0, FF, 256):
            hidden = gelu(wide).astype(BF)
            if at + 256 < FF:
                wide = dot(act[0:16, :], exp_v[:, at + 256:at + 512])
            temporal = temporal + dot(hidden, red_v[at:at + 256, :])

        for section in range(4):
            obuf[section] = temporal[8:16, 256 * section:256 * section + 256]
        for section in range(3):
            result_copy(section).start()
        out_ref[...] = obuf[3, MINE - 8:MINE - 8 + NF, :]
        for section in range(3):
            result_copy(section).wait_send()

    @pl.when(seg == 2)
    def _():
        for f in range(NF):
            for d in range(-REACH, REACH + 1):
                pool_copy(f, d).wait_send()

    @pl.when(seg < 2)
    def _():
        for f in range(NF):
            for c in range(BLOCKS):
                relay(f, c, 0, 1).wait_send()

    @pl.when(seg == 0)
    def _():
        for f in range(NF):
            early(f).wait_send()

    @pl.when(seg == 3)
    def _():
        for f in range(NF):
            for c in range(BLOCKS):
                relay(f, c, 1, 1).wait_send()

    @pl.when((seg == 0) & (core == 1))
    def _():
        for kind in range(2):
            shard(kind).wait_send()

    @pl.when(active)
    def _():
        half_drain()

    @pl.when(seg > 0)
    def _():
        full_drain()

    @pl.when(seg < 3)
    def _():
        result_copy(0).wait_recv()
        out_ref[...] = rbuf[MINE - 8:MINE - 8 + NF, :]


def body(frames, triple_weight, output_weight, expand_weight, reduce_weight, attend_gain, dense_gain, final_gain, shot_lengths):
    vmem = pl.BlockSpec(memory_space=pltpu.VMEM)
    anywhere = pl.BlockSpec(memory_space=pl.ANY)
    dma = pltpu.SemaphoreType.DMA
    return pl.pallas_call(
        kernel,
        out_shape=jax.ShapeDtypeStruct((NF, 256), F32),
        in_specs=[anywhere, anywhere, anywhere, anywhere, anywhere, vmem, vmem, vmem,
                  pl.BlockSpec(memory_space=pltpu.SMEM)],
        out_specs=vmem,
        scratch_shapes=[
            pltpu.VMEM((D, FF), BF), pltpu.VMEM((FF, D), BF),
            pltpu.VMEM((D, FF // 2), BF), pltpu.VMEM((FF // 2, D), BF), pltpu.VMEM((D, 3 * D), BF), pltpu.VMEM((D, D), BF),
            pltpu.VMEM((NF, ROWS, D), BF), pltpu.VMEM((PAD, FF), BF),
            pltpu.VMEM((NF, PAD, D), F32), pltpu.VMEM((2, NF, PAD, D), BF),
            pltpu.VMEM((NF, PAD, D), BF), pltpu.VMEM((NF, PAD, D), BF),
            pltpu.VMEM((PAD, 3 * D), BF), pltpu.VMEM((PAD, D), BF), pltpu.VMEM((PAD, D), BF),
            pltpu.VMEM((NF, 8, 128), F32), pltpu.VMEM((SLOTS, NF, 8, 128), F32), pltpu.VMEM((4, 8, 256), F32), pltpu.VMEM((8, 256), F32),
            dma((5,)), dma((2, 4, 4, 2)), dma((2, 4, 4, 2)), dma((2, 4, 4)), dma((2, 4, 4)),
            dma((2, 4, 4, 2)), dma((2, 4, 4, 2)), dma((2, 4, 4)), dma((2, 4, 4)),
            dma((NF, BLOCKS)), dma((2, NF, BLOCKS)), dma((NF,)), dma((NF,)), dma((2,)), dma((2,)),
            dma((NF, SLOTS)), dma((NF, SLOTS)), dma((3,)), dma(()),
        ],
        compiler_params=pltpu.CompilerParams(
            collective_id=0, has_side_effects=True, vmem_limit_bytes=60 * 1024 * 1024),
    )(frames, triple_weight, output_weight, expand_weight, reduce_weight, attend_gain, dense_gain,
      final_gain.reshape(1, D), shot_lengths)


def solution(mesh):
    return jax.shard_map(
        body,
        mesh=mesh,
        in_specs=(
            P("lane", None, None),
            P("segment", None, None),
            P("segment", None, None),
            P("segment", None, "lane"),
            P("segment", "lane", None),
            P("segment", None),
            P("segment", None),
            P(),
            P(),
        ),
        out_specs=P("lane", "segment"),
        check_vma=False,
    )
```

```python
import functools
import math

import jax
import jax.numpy as jnp
from jax import lax
from jax.experimental import pallas as pl
from jax.experimental.pallas import tpu as pltpu
from jax.sharding import PartitionSpec as P

HEADS = 16
ROWS = 197
PAD = 208
SENT = 200
BLOCKS = 2
WIDE = 1024 // BLOCKS
D = 1024
FF = 4096
NF = 3
REACH = 4
SLOTS = 2 * REACH + 1
KEYS = 32
MINE = NF * REACH
MESH = pl.DeviceIdType.MESH
F32 = jnp.float32
BF = jnp.bfloat16


def dot(a, b):
    return lax.dot_general(a, b, (((1,), (0,)), ((), ())), preferred_element_type=F32)


def dot_t(a, b):
    return lax.dot_general(a, b, (((1,), (1,)), ((), ())), preferred_element_type=F32)


def gelu(x):
    return 0.5 * x * (1.0 + lax.erf(x * (1.0 / math.sqrt(2.0))))


def norm_rows(x, gain):
    average = jnp.mean(x, axis=-1, keepdims=True)
    centred = x - average
    spread = jnp.mean(centred * centred, axis=-1, keepdims=True)
    return centred * lax.rsqrt(spread + 1e-06) * gain


def kernel(
    frames_hbm, triple_hbm, output_hbm, expand_hbm, reduce_hbm, again_ref, dgain_ref, fgain_ref, shot_ref,
    out_ref,
    exp_v, red_v, exp_h, red_h, trip_v, outw_v, frames_v, hid, state, inb, outb, outy, packed, act, ctx, pooled, pin, obuf, rbuf,
    local_sem, send_sem, recv_sem, sib_send, sib_recv, hsend_sem, hrecv_sem, hsib_send, hsib_recv,
    rel_send, rel_recv, early_send, early_recv, shard_send, shard_recv,
    pool_send, pool_recv, fin_send, fin_recv,
):
    seg = lax.axis_index("segment")
    lane = lax.axis_index("lane")
    cx = lane // 8
    cz = (lane // 2) % 4
    core = lane % 2

    def lane_at(x, z, c):
        return ((x % 4) * 4 + (z % 4)) * 2 + c

    loads = [
        pltpu.make_async_copy(triple_hbm.at[0], trip_v, local_sem.at[0]),
        pltpu.make_async_copy(output_hbm.at[0], outw_v, local_sem.at[1]),
        pltpu.make_async_copy(frames_hbm, frames_v, local_sem.at[4]),
    ]
    for copy in loads:
        copy.start()

    for f in range(NF):
        for way in range(2):
            inb[way, f, 192:PAD, :] = jnp.zeros((PAD - 192, D), BF)

    peers = [
        (seg, lane_at(cx + 1, cz, core)), (seg, lane_at(cx + 3, cz, core)),
        (seg, lane_at(cx, cz + 1, core)), (seg, lane_at(cx, cz + 3, core)),
        (seg, lane_at(cx, cz, 1 - core)),
        ((seg + 1) % 4, lane), ((seg + 3) % 4, lane),
    ]
    barrier = pltpu.get_barrier_semaphore()
    for peer in peers:
        pl.semaphore_signal(barrier, inc=1, device_id=peer, device_id_type=MESH)
    pl.semaphore_wait(barrier, len(peers))

    own_src = (expand_hbm.at[0], reduce_hbm.at[0])

    def pane(exp_ref, red_ref, kind, owner, half):
        if kind == 0:
            cols = pl.ds(pl.multiple_of(owner * 128, 128), 128)
            rows = pl.ds(0, D) if half is None else pl.ds(half * (D // 2), D // 2)
            return exp_ref.at[rows, cols]
        if half is None:
            return red_ref.at[pl.ds(pl.multiple_of(owner * 128, 128), 128), :]
        return red_ref.at[pl.ds(pl.multiple_of(owner * 128 + half * 64, 64), 64), :]

    def make_ring(exp_ref, red_ref, halved, ssem, rsem, bsend, brecv):
        def region(kind, dp, dq, c, half):
            x, z = (cx + dp + 4, cz + dq + 4) if kind == 0 else (cx + dq + 4, cz + dp + 4)
            owner = lane_at(x, z, 0) // 2 if halved else lane_at(x, z, c)
            return pane(exp_ref, red_ref, kind, owner, half)

        def neighbour(kind, along_p, sign):
            s = sign + 4
            if (kind == 0) == along_p:
                return (seg, lane_at(cx + s, cz, core))
            return (seg, lane_at(cx, cz + s, core))

        def source(kind, dp, dq, dst):
            return own_src[kind] if dp == 0 and dq == 0 and not halved else dst

        def hop(kind, dp, dq, half, along_p, sign):
            rp, rq = (dp - sign, dq) if along_p else (dp, dq - sign)
            h = half or 0
            dst = region(kind, dp, dq, core, half)
            return pltpu.make_async_remote_copy(
                src_ref=source(kind, dp, dq, dst), dst_ref=dst,
                send_sem=ssem.at[kind, rp % 4, rq % 4, h], recv_sem=rsem.at[kind, rp % 4, rq % 4, h],
                device_id=neighbour(kind, along_p, sign), device_id_type=MESH)

        def arrival(kind, rp, rq, half):
            h = half or 0
            dst = region(kind, rp, rq, core, half)
            return pltpu.make_async_remote_copy(
                src_ref=dst, dst_ref=dst,
                send_sem=ssem.at[kind, rp % 4, rq % 4, h], recv_sem=rsem.at[kind, rp % 4, rq % 4, h],
                device_id=neighbour(kind, True, 1), device_id_type=MESH)

        def sibling(kind, dp, dq, receive=False):
            dst = region(kind, dp, dq, 1 - core if receive else core, None)
            return pltpu.make_async_remote_copy(
                src_ref=dst if receive else source(kind, dp, dq, dst), dst_ref=dst,
                send_sem=bsend.at[kind, dp % 4, dq % 4], recv_sem=brecv.at[kind, dp % 4, dq % 4],
                device_id=(seg, lane_at(cx, cz, 1 - core)), device_id_type=MESH)

        sent = []

        def go(make, *args):
            make(*args).start()
            if (make, args) not in sent:
                sent.append((make, args))

        def start(ready=None):
            for kind in range(2):
                if ready is not None:
                    ready(kind)
                for sign in (1, -1):
                    go(hop, kind, 0, 0, None, True, sign)
                if ready is not None:
                    for sign in (1, -1):
                        go(hop, kind, 0, 0, None, False, sign)
            for kind in range(2):
                if ready is None:
                    for sign in (1, -1):
                        go(hop, kind, 0, 0, None, False, sign)
                go(sibling, kind, 0, 0)

        def spread(kind, dp):
            for sign in (1, -1):
                go(hop, kind, dp, 0, None, False, sign)
            go(sibling, kind, dp, 0)

        def ev_p(kind, rp):
            arrival(kind, rp, 0, None).wait_recv()
            go(hop, kind, rp, 0, 0 if rp < 0 else 1, True, -rp)
            spread(kind, rp)

        def ev_p2(kind):
            arrival(kind, 2, 0, 0).wait_recv()
            arrival(kind, 2, 0, 1).wait_recv()
            spread(kind, 2)

        def ev_q(kind, rp, rq):
            arrival(kind, rp, rq, None).wait_recv()
            go(hop, kind, rp, rq, 0 if rq < 0 else 1, False, -rq)
            go(sibling, kind, rp, rq)

        def ev_q2(kind, rp):
            arrival(kind, rp, 2, 0).wait_recv()
            arrival(kind, rp, 2, 1).wait_recv()
            go(sibling, kind, rp, 2)

        events = []

        def both(fn, *args):
            for kind in range(2):
                events.append(functools.partial(fn, kind, *args))

        both(ev_p, -1)
        both(ev_p, 1)
        both(ev_q, 0, -1)
        both(ev_q, 0, 1)
        both(ev_p2)
        both(ev_q, -1, -1)
        both(ev_q, -1, 1)
        both(ev_q, 1, -1)
        both(ev_q, 1, 1)
        both(ev_q2, 0)
        both(ev_q, 2, -1)
        both(ev_q, 2, 1)
        both(ev_q2, -1)
        both(ev_q2, 1)
        both(ev_q2, 2)

        def pump(count):
            for _ in range(min(count, len(events))):
                events.pop(0)()

        def from_sibling():
            for kind in range(2):
                for dp in range(4):
                    for dq in range(4):
                        sibling(kind, dp, dq, True).wait_recv()

        def drain():
            for make, args in sent:
                make(*args).wait_send()

        return start, pump, from_sibling, drain

    full_start, full_pump, full_sibling, full_drain = make_ring(
        exp_v, red_v, False, send_sem, recv_sem, sib_send, sib_recv)
    half_start, half_pump, half_sibling, half_drain = make_ring(
        exp_h, red_h, True, hsend_sem, hrecv_sem, hsib_send, hsib_recv)

    halves = (seg == 0) | (seg == 3)
    active = ((seg == 0) & (core == 0)) | ((seg == 3) & (core == 1))

    def shard(kind):
        return pltpu.make_async_remote_copy(
            src_ref=own_src[kind], dst_ref=pane(exp_h, red_h, kind, lane // 2, None),
            send_sem=shard_send.at[kind], recv_sem=shard_recv.at[kind],
            device_id=((seg + 3) % 4, lane), device_id_type=MESH)

    def own_load(kind, exp_ref, red_ref, owner):
        return pltpu.make_async_copy(own_src[kind], pane(exp_ref, red_ref, kind, owner, None), local_sem.at[2 + kind])

    @pl.when((seg == 0) & (core == 1))
    def _():
        for kind in range(2):
            shard(kind).start()

    @pl.when((seg == 0) & (core == 0))
    def _():
        for kind in range(2):
            own_load(kind, exp_h, red_h, lane // 2).start()

    def ready(kind):
        @pl.when(seg == 0)
        def _():
            own_load(kind, exp_h, red_h, lane // 2).wait()

        @pl.when(seg == 3)
        def _():
            shard(kind).wait_recv()

    @pl.when(active)
    def _():
        half_start(ready)

    def norm_into(f, gain_ref):
        gain = gain_ref[...]
        for i in range(PAD // 16):
            rows = pl.ds(16 * i, 16)
            act[rows, :] = norm_rows(state[f, rows, :], gain).astype(BF)

    def project(f):
        norm_into(f, again_ref)

        for at in range(0, 3 * D, 256):
            packed[:, at:at + 256] = dot(act[...], trip_v[:, at:at + 256]).astype(BF)

    def attend():
        low = lax.broadcasted_iota(jnp.int32, (PAD, 128), 1) < 64
        bias = jnp.where(lax.broadcasted_iota(jnp.int32, (1, PAD), 1) < ROWS, 0.0, -1e30).astype(F32)

        for at in range(0, D, 128):
            q = packed[:, at:at + 128]
            k = packed[:, D + at:D + at + 128]
            v = packed[:, 2 * D + at:2 * D + at + 128]
            parts = []
            for keep in (low, ~low):
                scores = dot_t(jnp.where(keep, q * 0.125, 0.0).astype(BF), k) + bias
                shares = jnp.exp(scores - jnp.max(scores, axis=-1, keepdims=True))
                total = jnp.sum(shares, axis=-1, keepdims=True)
                parts.append(dot(shares.astype(BF), v) / total)
            ctx[:, at:at + 128] = jnp.where(low, parts[0], parts[1]).astype(BF)

    def join(f):
        for at in range(0, D, 256):
            state[f, :, at:at + 256] += dot(ctx[...], outw_v[:, at:at + 256])

    def feed(f, exp_ref, red_ref, depth, emit):
        wide = dot(act[...], exp_ref[:, 0:256])
        for at in range(0, depth, 256):
            hidden = gelu(wide).astype(BF)
            if at + 256 < depth:
                wide = dot(act[...], exp_ref[:, at + 256:at + 512])
            hid[:, at:at + 256] = hidden
        for c in range(BLOCKS):
            cols = slice(WIDE * c, WIDE * c + WIDE)
            emit(c, cols, state[f, :, cols] + dot(hid[:, 0:depth], red_ref[:, cols]))

    def loaded():
        for copy in loads:
            copy.wait()

    def relay(f, c, way, section):
        cols = slice(WIDE * c, WIDE * c + WIDE)
        return pltpu.make_async_remote_copy(
            src_ref=outb.at[f, 0:SENT, cols], dst_ref=inb.at[way, f, 0:SENT, cols],
            send_sem=rel_send.at[f, c], recv_sem=rel_recv.at[way, f, c],
            device_id=(section, lane), device_id_type=MESH)

    def pass_on(f, way, section):
        def emit(c, cols, value):
            outb[f, :, cols] = value.astype(BF)
            relay(f, c, way, section).start()

        return emit

    def early(f):
        return pltpu.make_async_remote_copy(
            src_ref=outy.at[f, 0:SENT, :], dst_ref=inb.at[0, f, 0:SENT, :], send_sem=early_send.at[f], recv_sem=early_recv.at[f],
            device_id=((seg + 3) % 4, lane), device_id_type=MESH)

    @pl.when(halves)
    def _():
        loaded()
        for f in range(NF):
            @pl.when(seg == 0)
            def _():
                state[f, 192:PAD, :] = jnp.zeros((PAD - 192, D), F32)
                state[f, 0:ROWS, :] = frames_v[f].astype(F32)
                project(f)

            @pl.when(active)
            def _():
                half_pump(4)

            @pl.when(seg == 0)
            def _():
                attend()

            @pl.when(active)
            def _():
                half_pump(4)

            @pl.when(seg == 0)
            def _():
                join(f)
                norm_into(f, dgain_ref)
                outy[f] = act[...]
                early(f).start()

            @pl.when(active)
            def _():
                half_pump(2)

        @pl.when(active)
        def _():
            half_pump(1000)

        @pl.when(~active)
        def _():
            half_sibling()

        @pl.when(seg == 3)
        def _():
            full_start()

        def step(f, carry):
            @pl.when(seg == 3)
            def _():
                early(f).wait_recv()
                act[...] = inb[0, f]
                state[f] = jnp.zeros((PAD, D), F32)

            @pl.when(seg == 0)
            def _():
                act[...] = outy[f]

            feed(f, exp_h, red_h, FF // 2, pass_on(f, seg // 3, 1))
            return carry

        lax.fori_loop(0, NF, step, 0)

    @pl.when((seg == 1) | (seg == 2))
    def _():
        full_start()

    @pl.when(seg > 0)
    def _():
        for kind in range(2):
            own_load(kind, exp_v, red_v, lane).start()
        full_pump(1000)

    def gathered():
        full_sibling()
        for kind in range(2):
            own_load(kind, exp_v, red_v, lane).wait()

    def pool_copy(f, d):
        return pltpu.make_async_remote_copy(
            src_ref=pooled.at[f], dst_ref=pin.at[d + REACH, f],
            send_sem=pool_send.at[f, d + REACH], recv_sem=pool_recv.at[f, d + REACH],
            device_id=((seg + 1) % 4, (lane - d + 32) % 32), device_id_type=MESH)

    @pl.when((seg == 1) | (seg == 2))
    def _():
        loaded()

        def step(f, carry):
            for c in range(BLOCKS):
                relay(f, c, 0, 2).wait_recv()

            @pl.when(seg == 2)
            def _():
                state[f] = inb[0, f].astype(F32)

            @pl.when(seg == 1)
            def _():
                for c in range(BLOCKS):
                    relay(f, c, 1, 2).wait_recv()
                state[f] = inb[0, f].astype(F32) + inb[1, f].astype(F32)

            project(f)
            attend()
            join(f)
            norm_into(f, dgain_ref)

            @pl.when(f == 0)
            def _():
                gathered()

            @pl.when(seg == 1)
            def _():
                feed(f, exp_v, red_v, FF, pass_on(f, 0, 2))

            @pl.when(seg == 2)
            def _():
                def keep_block(c, cols, value):
                    state[f, :, cols] = value

                feed(f, exp_v, red_v, FF, keep_block)
                gain = fgain_ref[...]
                total = jnp.zeros((16, D), F32)
                for i in range(PAD // 16):
                    rows = norm_rows(state[f, pl.ds(16 * i, 16), :], gain)
                    if 16 * i + 16 > ROWS:
                        keep = lax.broadcasted_iota(jnp.int32, (16, D), 0) < ROWS - 16 * i
                        rows = jnp.where(keep, rows, 0.0)
                    total = total + rows
                total = jnp.sum(total, axis=0, keepdims=True) * (1.0 / ROWS)
                for j in range(8):
                    pooled[f, j:j + 1, :] = total[:, 128 * j:128 * j + 128]
                for d in range(-REACH, REACH + 1):
                    pool_copy(f, d).start()

            return carry

        lax.fori_loop(0, NF, step, 0)

    def result_copy(section):
        return pltpu.make_async_remote_copy(
            src_ref=obuf.at[section], dst_ref=rbuf, send_sem=fin_send.at[section], recv_sem=fin_recv,
            device_id=(section, lane), device_id_type=MESH)

    @pl.when(seg == 3)
    def _():
        state[0, 24:KEYS, :] = jnp.zeros((KEYS - 24, D), F32)
        for f in range(NF):
            for d in range(-REACH, REACH + 1):
                pool_copy(f, d).wait_recv()
                row = NF * (d + REACH) + f
                for j in range(8):
                    state[0, row:row + 1, 128 * j:128 * j + 128] = pin[d + REACH, f, j:j + 1, :]
        again = again_ref[...]
        for i in range(KEYS // 16):
            rows = pl.ds(16 * i, 16)
            act[rows, :] = norm_rows(state[0, rows, :], again).astype(BF)

        for at in range(0, 3 * D, 256):
            packed[0:KEYS, at:at + 256] = dot(act[0:KEYS, :], trip_v[:, at:at + 256]).astype(BF)

        col = lax.broadcasted_iota(jnp.int32, (16, KEYS), 1)
        row = lax.broadcasted_iota(jnp.int32, (16, KEYS), 0)
        key_at = (lane - REACH) * NF + col
        key_at = jnp.where(key_at < 0, key_at + 32 * NF, key_at)
        key_at = jnp.where(key_at >= 32 * NF, key_at - 32 * NF, key_at)
        own_at = lane * NF + jnp.clip(row - MINE, 0, NF - 1)
        key_shot = jnp.zeros((16, KEYS), jnp.int32)
        own_shot = jnp.zeros((16, KEYS), jnp.int32)
        end = 0
        for s in range(24):
            end = end + shot_ref[s]
            key_shot += (key_at >= end).astype(jnp.int32)
            own_shot += (own_at >= end).astype(jnp.int32)
        allowed = (key_shot == own_shot) & (col < NF * SLOTS)
        low = lax.broadcasted_iota(jnp.int32, (16, 128), 1) < 64

        for at in range(0, D, 128):
            q = packed[0:16, at:at + 128]
            k = packed[0:KEYS, D + at:D + at + 128]
            v = packed[0:KEYS, 2 * D + at:2 * D + at + 128]
            parts = []
            for keep in (low, ~low):
                scores = dot_t(jnp.where(keep, q * 0.125, 0.0).astype(BF), k)
                scores = jnp.where(allowed, scores, -1e30)
                shares = jnp.exp(scores - jnp.max(scores, axis=-1, keepdims=True))
                total = jnp.sum(shares, axis=-1, keepdims=True)
                high = shares.astype(BF)
                rest = (shares - high.astype(F32)).astype(BF)
                parts.append((dot(high, v) + dot(rest, v)) / total)
            ctx[0:16, at:at + 128] = jnp.where(low, parts[0], parts[1]).astype(BF)

        temporal = state[0, 0:16, :] + dot(ctx[0:16, :], outw_v[...])
        act[0:16, :] = norm_rows(temporal, dgain_ref[...]).astype(BF)

        gathered()
        wide = dot(act[0:16, :], exp_v[:, 0:256])
        for at in range(0, FF, 256):
            hidden = gelu(wide).astype(BF)
            if at + 256 < FF:
                wide = dot(act[0:16, :], exp_v[:, at + 256:at + 512])
            temporal = temporal + dot(hidden, red_v[at:at + 256, :])

        for section in range(4):
            obuf[section] = temporal[8:16, 256 * section:256 * section + 256]
        for section in range(3):
            result_copy(section).start()
        out_ref[...] = obuf[3, MINE - 8:MINE - 8 + NF, :]
        for section in range(3):
            result_copy(section).wait_send()

    @pl.when(seg == 2)
    def _():
        for f in range(NF):
            for d in range(-REACH, REACH + 1):
                pool_copy(f, d).wait_send()

    @pl.when(seg < 2)
    def _():
        for f in range(NF):
            for c in range(BLOCKS):
                relay(f, c, 0, 1).wait_send()

    @pl.when(seg == 0)
    def _():
        for f in range(NF):
            early(f).wait_send()

    @pl.when(seg == 3)
    def _():
        for f in range(NF):
            for c in range(BLOCKS):
                relay(f, c, 1, 1).wait_send()

    @pl.when((seg == 0) & (core == 1))
    def _():
        for kind in range(2):
            shard(kind).wait_send()

    @pl.when(active)
    def _():
        half_drain()

    @pl.when(seg > 0)
    def _():
        full_drain()

    @pl.when(seg < 3)
    def _():
        result_copy(0).wait_recv()
        out_ref[...] = rbuf[MINE - 8:MINE - 8 + NF, :]


def body(frames, triple_weight, output_weight, expand_weight, reduce_weight, attend_gain, dense_gain, final_gain, shot_lengths):
    vmem = pl.BlockSpec(memory_space=pltpu.VMEM)
    anywhere = pl.BlockSpec(memory_space=pl.ANY)
    dma = pltpu.SemaphoreType.DMA
    return pl.pallas_call(
        kernel,
        out_shape=jax.ShapeDtypeStruct((NF, 256), F32),
        in_specs=[anywhere, anywhere, anywhere, anywhere, anywhere, vmem, vmem, vmem,
                  pl.BlockSpec(memory_space=pltpu.SMEM)],
        out_specs=vmem,
        scratch_shapes=[
            pltpu.VMEM((D, FF), BF), pltpu.VMEM((FF, D), BF),
            pltpu.VMEM((D, FF // 2), BF), pltpu.VMEM((FF // 2, D), BF), pltpu.VMEM((D, 3 * D), BF), pltpu.VMEM((D, D), BF),
            pltpu.VMEM((NF, ROWS, D), BF), pltpu.VMEM((PAD, FF), BF),
            pltpu.VMEM((NF, PAD, D), F32), pltpu.VMEM((2, NF, PAD, D), BF),
            pltpu.VMEM((NF, PAD, D), BF), pltpu.VMEM((NF, PAD, D), BF),
            pltpu.VMEM((PAD, 3 * D), BF), pltpu.VMEM((PAD, D), BF), pltpu.VMEM((PAD, D), BF),
            pltpu.VMEM((NF, 8, 128), F32), pltpu.VMEM((SLOTS, NF, 8, 128), F32), pltpu.VMEM((4, 8, 256), F32), pltpu.VMEM((8, 256), F32),
            dma((5,)), dma((2, 4, 4, 2)), dma((2, 4, 4, 2)), dma((2, 4, 4)), dma((2, 4, 4)),
            dma((2, 4, 4, 2)), dma((2, 4, 4, 2)), dma((2, 4, 4)), dma((2, 4, 4)),
            dma((NF, BLOCKS)), dma((2, NF, BLOCKS)), dma((NF,)), dma((NF,)), dma((2,)), dma((2,)),
            dma((NF, SLOTS)), dma((NF, SLOTS)), dma((3,)), dma(()),
        ],
        compiler_params=pltpu.CompilerParams(
            collective_id=0, has_side_effects=True, vmem_limit_bytes=60 * 1024 * 1024),
    )(frames, triple_weight, output_weight, expand_weight, reduce_weight, attend_gain, dense_gain,
      final_gain.reshape(1, D), shot_lengths)


def solution(mesh):
    return jax.shard_map(
        body,
        mesh=mesh,
        in_specs=(
            P("lane", None, None),
            P("segment", None, None),
            P("segment", None, None),
            P("segment", None, "lane"),
            P("segment", "lane", None),
            P("segment", None),
            P("segment", None),
            P(),
            P(),
        ),
        out_specs=P("lane", "segment"),
        check_vma=False,
    )
```
